32 devices in a mesh: scan: 2 (over y), chan: 4 (over z), tm: 2 (over x), pol: 2 (over core).
Axes of the slice: x: 2, y: 2, z: 4, core: 2. Of those that a mesh axis runs over, the one named last changes fastest.
Arguments:
- samples: int32 [2, 8, 4, 2, 16, 32768], P('pol', ('scan', 'tm'), None, None, None, 'chan'), parts along dimension 1, may hold values from 0 to 3
- pcal_phase: float32 [2, 16, 128], P('pol'), may hold values from -3.140625 to 3.140625
- tone_index: int32 [32768], P('chan'), may hold values from 0 to 127
- baseline_pairs: int32 [120, 2], replicated, may hold values from 0 to 15, as said below
Outputs:
- fringe_power: float32 [2, 8, 120, 8192], P('pol', ('scan', 'chan'), 'tm'), parts along dimension 1
The draws below stay inside these ranges and needn't reach their ends.
There are 2 independent parts, one for each index of `scan`. The reference program is written for one: setup_inputs(seed, part) draws one part's arguments, and reference() takes and returns one part's arrays. A program takes and returns all parts, laid end to end along the dimension named above; an argument that names none is the same for every part. Nothing has to cross between parts.
Inputs may be any that keep to these rules, and one draw needn't show every extreme that they name: `baseline_pairs`: each row holds two different stations; every unordered pair of the 16 stations stands in exactly one row, in either order.
All inputs are finite; a program needn't handle non-finite values.
Results may differ from the reference program's by a relative error of at most 0.0029.
Values may be sent and summed in bfloat16 or wider, within the bound.
No kernel may reach another device: no remote copies, remote signals or barrier semaphores. Data moves between devices by JAX's collectives and lax.ppermute only.
A program may use at most 256 MiB of HBM per device.

```python
import jax
import jax.numpy as jnp
import numpy as np
from jax import lax

S = 16
NC = 32768
NTONE = 128
M = 4
NPOL = 2
NT = 4
ND = 8192


def draw_baseline_pairs(key, part):
    pair_table = np.array([(low_station, high_station) for low_station in range(S) for high_station in range(low_station + 1, S)], dtype=np.int32)
    pair_order = jax.random.permutation(key, pair_table.shape[0])
    picked_rows = jnp.asarray(pair_table)[pair_order]
    flipped = jax.random.randint(jax.random.fold_in(key, 7), (pair_table.shape[0],), 0, 2)
    first_station = jnp.where(flipped == 1, picked_rows[:, 1], picked_rows[:, 0])
    second_station = jnp.where(flipped == 1, picked_rows[:, 0], picked_rows[:, 1])
    return jnp.stack([first_station, second_station], axis=1).astype(jnp.int32)


def with_ends(result, stream_key, smallest, high):
    longest = result.shape.index(max(result.shape))
    spots = []
    for shift in (0, 1):
        where = [jax.random.randint(jax.random.fold_in(stream_key, axis), (), 0, length) for axis, length in enumerate(result.shape)]
        where[longest] = (where[longest] + shift) % result.shape[longest]
        spots.append(tuple(where))
    return result.at[spots[0]].set(smallest).at[spots[1]].set(high)


def setup_inputs(seed: int = 0, part: int = 0) -> dict:
    seeds = jax.random.split(jax.random.key(seed), 5)
    part_splits = jax.random.split(jax.random.fold_in(seeds[4], part), 5)
    return {
        "samples": with_ends(jax.random.randint(part_splits[0], (NPOL, NT, M, 2, S, NC), 0, 4), jax.random.fold_in(part_splits[0], 1), 0, 3).astype(jnp.int32),
        "pcal_phase": jnp.clip(jax.random.uniform(seeds[1], (NPOL, S, NTONE), jnp.float32, -3.140625, 3.140625), -3.140625, 3.140625),
        "tone_index": with_ends(jax.random.randint(seeds[2], (NC,), 0, NTONE), jax.random.fold_in(seeds[2], 1), 0, NTONE - 1).astype(jnp.int32),
        "baseline_pairs": draw_baseline_pairs(jax.random.fold_in(seeds[4], 71), part),
    }


def calibrated_period(block, first_index, second_index, cos_diff, sin_diff):
    levels = (2 * block - 3).astype(jnp.float32)
    first_volts = levels[:, :, first_index, :]
    second_volts = levels[:, :, second_index, :]
    raw_real = jnp.sum(first_volts[:, 0] * second_volts[:, 0] + first_volts[:, 1] * second_volts[:, 1], axis=0)
    raw_imag = jnp.sum(first_volts[:, 1] * second_volts[:, 0] - first_volts[:, 0] * second_volts[:, 1], axis=0)
    vis_real = raw_real * cos_diff + raw_imag * sin_diff
    vis_imag = raw_imag * cos_diff - raw_real * sin_diff
    return jnp.stack([vis_real, vis_imag], axis=1).astype(jnp.bfloat16)


def one_polarization(samples_pol, phase_pol, tone_index, baseline_pairs):
    first_index = baseline_pairs[:, 0]
    second_index = baseline_pairs[:, 1]
    cos_table = jnp.cos(phase_pol)[:, tone_index]
    sin_table = jnp.sin(phase_pol)[:, tone_index]
    cos_first = cos_table[first_index]
    sin_first = sin_table[first_index]
    cos_second = cos_table[second_index]
    sin_second = sin_table[second_index]
    cos_diff = cos_first * cos_second + sin_first * sin_second
    sin_diff = sin_first * cos_second - cos_first * sin_second

    def per_period(block):
        return calibrated_period(block, first_index, second_index, cos_diff, sin_diff)

    visibility = lax.map(per_period, samples_pol)
    values = visibility.astype(jnp.float32)
    spectra = jnp.fft.fft(lax.complex(values[:, :, 0], values[:, :, 1]), axis=0)
    lag_index = (jnp.arange(ND, dtype=jnp.int32) - ND // 2) % NC
    scale = 1.0 / (100.0 * M * NT * NC)

    def per_rate(rate_row):
        delays = jnp.fft.fft(rate_row, axis=-1)[:, lag_index]
        return (jnp.real(delays) * jnp.real(delays) + jnp.imag(delays) * jnp.imag(delays)) * scale

    return lax.map(per_rate, spectra)


def reference(samples, pcal_phase, tone_index, baseline_pairs):
    outputs = [one_polarization(samples[pol_index], pcal_phase[pol_index], tone_index, baseline_pairs) for pol_index in range(NPOL)]
    return jnp.stack(outputs, axis=0).astype(jnp.float32)
```

```python
import functools
import math

import jax
import jax.numpy as jnp
import numpy as np
from jax import lax
from jax.experimental import pallas as pl
from jax.experimental.pallas import tpu as pltpu
from jax.sharding import PartitionSpec as P

LANES = 128
NTONE = 128
N_DELAY = 8192
CHUNKS = 5
two_pi = 2.0 * math.pi
bf16 = jnp.bfloat16
f32 = jnp.float32


def split_bf16(values):
    high = values.astype(bf16)
    return high, (values - high.astype(f32)).astype(bf16)


def np_split(values):
    values = np.asarray(values, np.float32)
    high = values.astype(bf16)
    return high, (values - high.astype(np.float32)).astype(bf16)


def np_phase(left, right, modulus):
    product = np.outer(left, right).astype(np.int64) % modulus
    angles = two_pi * product / modulus
    return np.cos(angles), np.sin(angles)


def prep_kernel(samples_ref, tone_ref, table_ref, lev_ref, cal_ref, scratch):
    _, n_t, n_m, _, n_s, width = samples_ref.shape
    rows = width // LANES

    def regroup(block):
        for row in range(rows):
            scratch[pl.ds(row, n_s, stride=rows), :] = block[:, row * LANES : (row + 1) * LANES]
        return scratch[...].reshape(n_s, rows, LANES)

    for t in range(n_t):
        for m in range(n_m):
            for p in range(2):
                level = (2 * samples_ref[0, t, m, p] - 3).astype(f32)
                lev_ref[t, m, p] = regroup(level).astype(bf16)
    slots = lax.broadcasted_iota(jnp.int32, (NTONE, width), 0)
    hot = jnp.where(slots == tone_ref[...], 1.0, 0.0).astype(bf16)
    parts = jnp.dot(table_ref[...], hot, preferred_element_type=f32)
    for p in range(2):
        first = parts[(3 * p) * n_s : (3 * p + 1) * n_s]
        second = parts[(3 * p + 1) * n_s : (3 * p + 2) * n_s]
        third = parts[(3 * p + 2) * n_s : (3 * p + 3) * n_s]
        cal_ref[p] = regroup((first + second) + third)


def prep(samples, tone_index, pcal_phase):
    _, n_t, n_m, _, n_s, n_c = samples.shape
    width = min(n_c, 2048)
    rows = width // LANES
    parts = []
    for table in (jnp.cos(pcal_phase[0]), jnp.sin(pcal_phase[0])):
        high = lax.reduce_precision(table, 8, 7)
        middle = lax.reduce_precision(table - high, 8, 7)
        parts += [high, middle, (table - high) - middle]
    tables = jnp.concatenate(parts, axis=0).astype(bf16)
    return pl.pallas_call(
        prep_kernel,
        grid=(n_c // width,),
        in_specs=[
            pl.BlockSpec((1, n_t, n_m, 2, n_s, width), lambda i: (0, 0, 0, 0, 0, i)),
            pl.BlockSpec((1, width), lambda i: (0, i)),
            pl.BlockSpec((6 * n_s, NTONE), lambda i: (0, 0)),
        ],
        out_specs=[
            pl.BlockSpec((n_t, n_m, 2, n_s, rows, LANES), lambda i: (0, 0, 0, 0, i, 0)),
            pl.BlockSpec((2, n_s, rows, LANES), lambda i: (0, 0, i, 0)),
        ],
        out_shape=[
            jax.ShapeDtypeStruct((n_t, n_m, 2, n_s, n_c // LANES, LANES), bf16),
            jax.ShapeDtypeStruct((2, n_s, n_c // LANES, LANES), f32),
        ],
        scratch_shapes=[pltpu.VMEM((n_s * rows, LANES), f32)],
        name="prep",
    )(samples, tone_index[None, :], tables)


def visibility_rows(lev_ref, cal_ref, first, second, rows):
    n_t, n_m = lev_ref.shape[:2]
    cos_a, sin_a = cal_ref[0, first, rows], cal_ref[1, first, rows]
    cos_e, sin_e = cal_ref[0, second, rows], cal_ref[1, second, rows]
    cos_diff = cos_a * cos_e + sin_a * sin_e
    sin_diff = sin_a * cos_e - cos_a * sin_e
    result = []
    for t in range(n_t):
        real, imag = None, None
        for m in range(n_m):
            ar, ai = lev_ref[t, m, 0, first, rows], lev_ref[t, m, 1, first, rows]
            er, ei = lev_ref[t, m, 0, second, rows], lev_ref[t, m, 1, second, rows]
            re = ar * er + ai * ei
            im = ai * er - ar * ei
            real = re if real is None else real + re
            imag = im if imag is None else imag + im
        real, imag = real.astype(f32), imag.astype(f32)
        vis_real = real * cos_diff + imag * sin_diff
        vis_imag = imag * cos_diff - real * sin_diff
        result.append((vis_real.astype(bf16), vis_imag.astype(bf16)))
    return result


def corr_kernel(start_ref, pairs_ref, lev_ref, cal_ref, out_ref):
    baseline = start_ref[0] + pl.program_id(0)
    first, second = pairs_ref[baseline, 0], pairs_ref[baseline, 1]
    n_rows = lev_ref.shape[4]
    step = min(16, n_rows)
    for base in range(0, n_rows, step):
        rows = slice(base, base + step)
        for t, (real, imag) in enumerate(visibility_rows(lev_ref, cal_ref, first, second, rows)):
            out_ref[0, t, 0, rows] = real
            out_ref[0, t, 1, rows] = imag


def resident(array):
    rank = array.ndim
    return pl.BlockSpec(array.shape, lambda *_: (0,) * rank, pipeline_mode=pl.Buffered(1))


def correlate(levels, cal, pairs, start, count):
    n_t = levels.shape[0]
    shape = (n_t, 2) + levels.shape[4:]
    return pl.pallas_call(
        corr_kernel,
        grid_spec=pltpu.PrefetchScalarGridSpec(
            num_scalar_prefetch=2,
            grid=(count,),
            in_specs=[resident(levels), resident(cal)],
            out_specs=pl.BlockSpec((1,) + shape, lambda i, *_: (i, 0, 0, 0, 0)),
        ),
        out_shape=jax.ShapeDtypeStruct((count,) + shape, bf16),
        name="correlate",
    )(start[None], pairs, levels, cal)


def weighted(terms):
    total = None
    for weight, value in terms:
        if weight == 0.0:
            continue
        value = value if abs(weight) == 1.0 else abs(weight) * value
        if total is None:
            total = value if weight > 0 else -value
        else:
            total = total + value if weight > 0 else total - value
    return total


def clean(value):
    rounded = round(value)
    return float(rounded) if abs(value - rounded) < 1e-12 else float(value)


def rate_kernel(quant, start_ref, pairs_ref, lev_ref, cal_ref, *refs):
    received, out_ref = refs[:-1], refs[-1]
    n_rates = out_ref.shape[0]
    baseline = start_ref[0] + pl.program_id(0)
    first, second = pairs_ref[baseline, 0], pairs_ref[baseline, 1]
    n_rows = lev_ref.shape[4]
    step = min(16, n_rows)
    for base in range(0, n_rows, step):
        rows = slice(base, base + step)
        periods = list(visibility_rows(lev_ref, cal_ref, first, second, rows))
        for ref in received:
            for t in range(ref.shape[1]):
                periods.append((ref[0, t, 0, rows], ref[0, t, 1, rows]))
        periods = [(real.astype(f32), imag.astype(f32)) for real, imag in periods]
        for r in range(n_rates):
            real_terms, imag_terms = [], []
            for t, (real, imag) in enumerate(periods):
                angle = two_pi * ((r * t) % n_rates) / n_rates
                cosine, sine = clean(math.cos(angle)), clean(math.sin(angle))
                real_terms += [(cosine, real), (sine, imag)]
                imag_terms += [(cosine, imag), (-sine, real)]
            for p, terms in enumerate((real_terms, imag_terms)):
                value = jnp.round(weighted(terms) * quant)
                out_ref[r, 0, p, rows] = value.astype(jnp.int32).astype(jnp.int16)


def rates(levels, cal, pairs, start, received, quant, n_rates):
    count = received[0].shape[0]
    shape = (2,) + levels.shape[4:]
    return pl.pallas_call(
        functools.partial(rate_kernel, quant),
        grid_spec=pltpu.PrefetchScalarGridSpec(
            num_scalar_prefetch=2,
            grid=(count,),
            in_specs=[resident(levels), resident(cal)]
            + [pl.BlockSpec((1,) + r.shape[1:], lambda i, *_: (i, 0, 0, 0, 0)) for r in received],
            out_specs=pl.BlockSpec((n_rates, 1) + shape, lambda i, *_: (0, i, 0, 0, 0)),
        ),
        out_shape=jax.ShapeDtypeStruct((n_rates, count) + shape, jnp.int16),
        name="rates",
    )(start[None], pairs, levels, cal, *received)


def delay_kernel(scale, spec_ref, first_ref, twist_ref, last_ref, out_ref):
    n_src, group, _, rows, _ = spec_ref.shape
    outer = n_src * rows
    kept = last_ref.shape[0] // 2
    highs, lows = [], []
    for p in range(2):
        pieces = [
            split_bf16(spec_ref[:, g, p].astype(jnp.int32).astype(f32).reshape(outer, LANES))
            for g in range(group)
        ]
        highs.append(jnp.concatenate([piece[0] for piece in pieces], axis=1))
        lows.append(jnp.concatenate([piece[1] for piece in pieces], axis=1))
    high = jnp.concatenate(highs, axis=0)
    low = jnp.concatenate(lows, axis=0)
    stacked = jnp.concatenate([high, high, low], axis=0)
    section = jnp.dot(first_ref[...], stacked, preferred_element_type=f32)
    for g in range(group):
        real = section[:outer, g * LANES : (g + 1) * LANES]
        imag = section[outer:, g * LANES : (g + 1) * LANES]
        twist_cos, twist_sin = twist_ref[0], twist_ref[1]
        twisted = [real * twist_cos + imag * twist_sin, imag * twist_cos - real * twist_sin]
        parts = [split_bf16(value) for value in twisted]
        t_high = jnp.concatenate([parts[0][0], parts[1][0]], axis=1)
        t_low = jnp.concatenate([parts[0][1], parts[1][1]], axis=1)
        operand = jnp.concatenate([t_high, t_low, t_high], axis=1)
        final = lax.dot_general(
            last_ref[...], operand, (((1,), (1,)), ((), ())), preferred_element_type=f32
        )
        real, imag = final[:kept], final[kept:]
        out_ref[g] = (real * real + imag * imag) * scale


def delay_tables(n_chan_total, kept_rows):
    outer = n_chan_total // LANES
    cos1, sin1 = np_phase(np.arange(outer), np.arange(outer), outer)
    first = np.block([[cos1, sin1], [-sin1, cos1]])
    high, low = np_split(first)
    first = np.concatenate([high, low, high], axis=1)
    cos_t, sin_t = np_phase(np.arange(outer), np.arange(LANES), n_chan_total)
    twist = np.stack([cos_t, sin_t]).astype(np.float32)
    kept = np.arange(-(kept_rows // 2), kept_rows - kept_rows // 2)
    cos2, sin2 = np_phase(kept, np.arange(LANES), LANES)
    last = np.block([[cos2, sin2], [-sin2, cos2]])
    high, low = np_split(last)
    last = np.concatenate([high, high, low], axis=1)
    return first, twist, last


def delays(spectra, tables, scale, kept_rows):
    n_src, count, _, rows, _ = spectra.shape
    outer = n_src * rows
    group = 2 if count % 2 == 0 else 1
    first, twist, last = [jnp.asarray(table) for table in tables]
    return pl.pallas_call(
        functools.partial(delay_kernel, scale),
        grid=(count // group,),
        in_specs=[
            pl.BlockSpec((n_src, group, 2, rows, LANES), lambda i: (0, i, 0, 0, 0)),
            resident(first),
            resident(twist),
            resident(last),
        ],
        out_specs=pl.BlockSpec((group, kept_rows, outer), lambda i: (i, 0, 0)),
        out_shape=jax.ShapeDtypeStruct((count, kept_rows, outer), f32),
        name="delays",
    )(spectra, first, twist, last)


def shards(samples, pcal_phase, tone_index, baseline_pairs):
    n_tm = lax.axis_size("tm")
    n_chan = lax.axis_size("chan")
    n_t, n_m = samples.shape[1:3]
    n_rates = n_t * n_tm
    per_rate = n_rates // n_chan
    channels = samples.shape[5] * n_chan
    outer = channels // LANES
    kept_rows = N_DELAY // outer
    count = baseline_pairs.shape[0] // n_tm
    chunks = CHUNKS if count % CHUNKS == 0 else 1
    size = count // chunks
    me = lax.axis_index("tm")
    bound = 18.0 * n_m * n_rates
    quant = 32767.0 / bound
    scale = 1.0 / (100.0 * n_m * n_rates * channels) / (quant * quant)
    tables = delay_tables(channels, kept_rows)

    levels, cal = prep(samples, tone_index, pcal_phase)
    powers = []
    for chunk in range(chunks):
        received = []
        for shift in range(1, n_tm):
            target = lax.rem(me + (n_tm - shift), n_tm)
            block = correlate(levels, cal, baseline_pairs, target * count + chunk * size, size)
            hops = [(j, (j - shift) % n_tm) for j in range(n_tm)]
            received.append(lax.ppermute(block, "tm", hops))
        spectra = rates(
            levels, cal, baseline_pairs, me * count + chunk * size, received, quant, n_rates
        )
        gathered = lax.all_to_all(spectra, "chan", split_axis=0, concat_axis=0, tiled=True)
        gathered = gathered.reshape((n_chan, per_rate * size) + gathered.shape[2:])
        power = delays(gathered, tables, scale, kept_rows)
        powers.append(power.reshape(per_rate, size, N_DELAY))
    power = jnp.concatenate(powers, axis=1) if chunks > 1 else powers[0]
    return power[None]


def solution(mesh):
    placed = (
        P("pol", ("scan", "tm"), None, None, None, "chan"),
        P("pol", None, None),
        P("chan"),
        P(),
    )
    return jax.shard_map(
        shards,
        mesh=mesh,
        in_specs=placed,
        out_specs=P("pol", ("scan", "chan"), "tm", None),
        check_vma=False,
    )
```

```python
import functools
import math

import jax
import jax.numpy as jnp
import numpy as np
from jax import lax
from jax.experimental import pallas as pl
from jax.experimental.pallas import tpu as pltpu
from jax.sharding import PartitionSpec as P


LANES = 128
NTONE = 128
N_DELAY = 8192
CHUNKS = 5
COST_SCALE = 2.0e6
VMEM_GRANT = 24 * 2**20
two_pi = 2.0 * math.pi
bf16 = jnp.bfloat16
f32 = jnp.float32


def split_bf16(values):
    high = values.astype(bf16)
    return high, (values - high.astype(f32)).astype(bf16)


def np_split(values):
    values = np.asarray(values, np.float32)
    high = values.astype(bf16)
    return high, (values - high.astype(np.float32)).astype(bf16)


def np_phase(left, right, modulus):
    product = np.outer(left, right).astype(np.int64) % modulus
    angles = two_pi * product / modulus
    return np.cos(angles), np.sin(angles)


def prep_kernel(samples_ref, tone_ref, table_ref, lev_ref, cal_ref, scratch):
    _, n_t, n_m, _, n_s, width = samples_ref.shape
    rows = width // LANES

    def regroup(block):
        for row in range(rows):
            scratch[pl.ds(row, n_s, stride=rows), :] = block[:, row * LANES : (row + 1) * LANES]
        return scratch[...].reshape(n_s, rows, LANES)

    for t in range(n_t):
        for m in range(n_m):
            for p in range(2):
                level = (2 * samples_ref[0, t, m, p] - 3).astype(f32)
                lev_ref[t, m, p] = regroup(level).astype(bf16)
    slots = lax.broadcasted_iota(jnp.int32, (NTONE, width), 0)
    hot = jnp.where(slots == tone_ref[...], 1.0, 0.0).astype(bf16)
    parts = jnp.dot(table_ref[...], hot, preferred_element_type=f32)
    for p in range(2):
        first = parts[(3 * p) * n_s : (3 * p + 1) * n_s]
        second = parts[(3 * p + 1) * n_s : (3 * p + 2) * n_s]
        third = parts[(3 * p + 2) * n_s : (3 * p + 3) * n_s]
        cal_ref[p] = regroup((first + second) + third)


def prep(samples, tone_index, pcal_phase):
    _, n_t, n_m, _, n_s, n_c = samples.shape
    width = min(n_c, 2048)
    rows = width // LANES
    parts = []
    for table in (jnp.cos(pcal_phase[0]), jnp.sin(pcal_phase[0])):
        high = lax.reduce_precision(table, 8, 7)
        middle = lax.reduce_precision(table - high, 8, 7)
        parts += [high, middle, (table - high) - middle]
    tables = jnp.concatenate(parts, axis=0).astype(bf16)
    return pl.pallas_call(
        prep_kernel,
        grid=(n_c // width,),
        in_specs=[
            pl.BlockSpec((1, n_t, n_m, 2, n_s, width), lambda i: (0, 0, 0, 0, 0, i)),
            pl.BlockSpec((1, width), lambda i: (0, i)),
            pl.BlockSpec((6 * n_s, NTONE), lambda i: (0, 0)),
        ],
        out_specs=[
            pl.BlockSpec((n_t, n_m, 2, n_s, rows, LANES), lambda i: (0, 0, 0, 0, i, 0)),
            pl.BlockSpec((2, n_s, rows, LANES), lambda i: (0, 0, i, 0)),
        ],
        out_shape=[
            jax.ShapeDtypeStruct((n_t, n_m, 2, n_s, n_c // LANES, LANES), bf16),
            jax.ShapeDtypeStruct((2, n_s, n_c // LANES, LANES), f32),
        ],
        scratch_shapes=[pltpu.VMEM((n_s * rows, LANES), f32)],
        compiler_params=pltpu.CompilerParams(vmem_limit_bytes=VMEM_GRANT),
        name="prep",
    )(samples, tone_index[None, :], tables)


def visibility_rows(lev_ref, cal_ref, first, second, rows):
    n_t, n_m = lev_ref.shape[:2]
    cos_a, sin_a = cal_ref[0, first, rows], cal_ref[1, first, rows]
    cos_e, sin_e = cal_ref[0, second, rows], cal_ref[1, second, rows]
    cos_diff = cos_a * cos_e + sin_a * sin_e
    sin_diff = sin_a * cos_e - cos_a * sin_e
    result = []
    for t in range(n_t):
        real, imag = None, None
        for m in range(n_m):
            ar, ai = lev_ref[t, m, 0, first, rows], lev_ref[t, m, 1, first, rows]
            er, ei = lev_ref[t, m, 0, second, rows], lev_ref[t, m, 1, second, rows]
            re = ar * er + ai * ei
            im = ai * er - ar * ei
            real = re if real is None else real + re
            imag = im if imag is None else imag + im
        real, imag = real.astype(f32), imag.astype(f32)
        vis_real = real * cos_diff + imag * sin_diff
        vis_imag = imag * cos_diff - real * sin_diff
        result.append((vis_real.astype(bf16), vis_imag.astype(bf16)))
    return result


def vmem():
    return pl.BlockSpec(memory_space=pltpu.VMEM)


def smem():
    return pl.BlockSpec(memory_space=pltpu.SMEM)


def cost(micros):
    return pl.CostEstimate(flops=0, bytes_accessed=int(micros * COST_SCALE), transcendentals=0)


def corr_kernel(start_ref, pairs_ref, lev_ref, cal_ref, out_ref):
    n_rows = lev_ref.shape[4]
    step = min(16, n_rows)

    def body(index, carry):
        baseline = start_ref[0] + index
        first, second = pairs_ref[baseline, 0], pairs_ref[baseline, 1]
        for base in range(0, n_rows, step):
            rows = slice(base, base + step)
            for t, (real, imag) in enumerate(
                visibility_rows(lev_ref, cal_ref, first, second, rows)
            ):
                out_ref[index, t, 0, rows] = real
                out_ref[index, t, 1, rows] = imag
        return carry

    lax.fori_loop(0, out_ref.shape[0], body, 0)


def correlate(levels, cal, pairs, start, count):
    n_t = levels.shape[0]
    shape = (n_t, 2) + levels.shape[4:]
    return pl.pallas_call(
        corr_kernel,
        in_specs=[smem(), smem(), vmem(), vmem()],
        out_specs=vmem(),
        out_shape=jax.ShapeDtypeStruct((count,) + shape, bf16),
        cost_estimate=cost(3),
        compiler_params=pltpu.CompilerParams(vmem_limit_bytes=VMEM_GRANT),
        name="correlate",
    )(start[None], pairs, levels, cal)


def weighted(terms):
    total = None
    for weight, value in terms:
        if weight == 0.0:
            continue
        value = value if abs(weight) == 1.0 else abs(weight) * value
        if total is None:
            total = value if weight > 0 else -value
        else:
            total = total + value if weight > 0 else total - value
    return total


def clean(value):
    rounded = round(value)
    return float(rounded) if abs(value - rounded) < 1e-12 else float(value)


def rate_kernel(quant, start_ref, pairs_ref, turn_ref, lev_ref, cal_ref, *refs):
    n_rates = turn_ref.shape[0]
    received, outs = refs[:-n_rates], refs[-n_rates:]
    n_rows = lev_ref.shape[4]
    step = min(16, n_rows)

    def body(index, carry):
        baseline = start_ref[0] + index
        first, second = pairs_ref[baseline, 0], pairs_ref[baseline, 1]
        for base in range(0, n_rows, step):
            rows = slice(base, base + step)
            periods = list(visibility_rows(lev_ref, cal_ref, first, second, rows))
            for ref in received:
                for t in range(ref.shape[1]):
                    periods.append((ref[index, t, 0, rows], ref[index, t, 1, rows]))
            turned = []
            for t, (real, imag) in enumerate(periods):
                real, imag = real.astype(f32), imag.astype(f32)
                if t == 0:
                    turned.append((real * quant, imag * quant))
                    continue
                cosine, sine = turn_ref[t, 0] * quant, turn_ref[t, 1] * quant
                turned.append((real * cosine + imag * sine, imag * cosine - real * sine))
            for pair, out_ref in zip(small_dft(turned), outs):
                for p, value in enumerate(pair):
                    out_ref[index, p, rows] = jnp.round(value).astype(jnp.int32).astype(jnp.int16)
        return carry

    lax.fori_loop(0, outs[0].shape[0], body, 0)


def small_dft(values):
    count = len(values)
    if count % 2 == 0:
        even, odd = small_dft(values[0::2]), small_dft(values[1::2])
        result = [None] * count
        for k in range(count // 2):
            angle = two_pi * k / count
            cosine, sine = clean(math.cos(angle)), clean(math.sin(angle))
            (er, ei), (odd_r, odd_i) = even[k], odd[k]
            tr = weighted([(cosine, odd_r), (sine, odd_i)])
            ti = weighted([(cosine, odd_i), (-sine, odd_r)])
            result[k] = (er + tr, ei + ti)
            result[k + count // 2] = (er - tr, ei - ti)
        return result
    result = []
    for k in range(count):
        real_terms, imag_terms = [], []
        for t, (real, imag) in enumerate(values):
            angle = two_pi * ((k * t) % count) / count
            cosine, sine = clean(math.cos(angle)), clean(math.sin(angle))
            real_terms += [(cosine, real), (sine, imag)]
            imag_terms += [(cosine, imag), (-sine, real)]
        result.append((weighted(real_terms), weighted(imag_terms)))
    return result


def rates(levels, cal, pairs, start, turn, received, quant):
    count = received[0].shape[0]
    shape = (count, 2) + levels.shape[4:]
    n_rates = turn.shape[0]
    return pl.pallas_call(
        functools.partial(rate_kernel, quant),
        in_specs=[smem(), smem(), smem(), vmem(), vmem()] + [vmem() for _ in received],
        out_specs=[vmem()] * n_rates,
        out_shape=[jax.ShapeDtypeStruct(shape, jnp.int16)] * n_rates,
        cost_estimate=cost(4),
        compiler_params=pltpu.CompilerParams(vmem_limit_bytes=VMEM_GRANT),
        name="rates",
    )(start[None], pairs, turn, levels, cal, *received)


def delay_kernel(scale, n_src, first_ref, twist_ref, last_ref, *refs):
    specs = refs[:n_src]
    out_ref, real_scratch, imag_scratch = refs[-3:]
    total, _, rows, _ = specs[0].shape
    outer = n_src * rows
    kept = last_ref.shape[0] // 2
    group = real_scratch.shape[0]
    halves = outer // LANES

    def body(step, carry):
        sources = []
        for src in range(n_src):
            pair = []
            for p in range(2):
                lanes = [
                    specs[src][step * group + g, p].astype(jnp.int32).astype(f32)
                    for g in range(group)
                ]
                pair.append(jnp.concatenate(lanes, axis=1))
            sources.append(tuple(pair))
        for low_digit, (real, imag) in enumerate(small_dft([sources[0]] + sources[:0:-1])):
            real_parts, imag_parts = split_bf16(real), split_bf16(imag)
            high = jnp.concatenate([real_parts[0], imag_parts[0]], axis=0)
            low = jnp.concatenate([real_parts[1], imag_parts[1]], axis=0)
            stacked = jnp.concatenate([high, low, high], axis=0)
            section = jnp.dot(first_ref[low_digit], stacked, preferred_element_type=f32)
            twist_cos, twist_sin = twist_ref[0, low_digit], twist_ref[1, low_digit]
            for g in range(group):
                real = section[:rows, g * LANES : (g + 1) * LANES]
                imag = section[rows:, g * LANES : (g + 1) * LANES]
                place = pl.ds(low_digit, rows, stride=n_src)
                real_scratch[g, place, :] = real * twist_cos + imag * twist_sin
                imag_scratch[g, place, :] = imag * twist_cos - real * twist_sin
        for g in range(group):
            real_parts = split_bf16(real_scratch[g])
            imag_parts = split_bf16(imag_scratch[g])
            high = jnp.concatenate([real_parts[0], imag_parts[0]], axis=1)
            low = jnp.concatenate([real_parts[1], imag_parts[1]], axis=1)
            operand = jnp.concatenate([high, low, high], axis=1)
            final = lax.dot_general(
                last_ref[...], operand, (((1,), (1,)), ((), ())), preferred_element_type=f32
            )
            real, imag = final[:kept], final[kept:]
            power = (real * real + imag * imag) * scale
            for half in range(halves):
                out_ref[step * group + g, pl.ds(half, kept, stride=halves), :] = power[
                    :, half * LANES : (half + 1) * LANES
                ]
        return carry

    lax.fori_loop(0, total // group, body, 0)


def delay_tables(n_chan_total, kept_rows, n_src):
    outer = n_chan_total // LANES
    local = outer // n_src
    firsts, twists = [], []
    for low_digit in range(n_src):
        d = n_src * np.arange(local) + low_digit
        cos1, sin1 = np_phase(d, np.arange(local), outer)
        high, low = np_split(np.block([[cos1, sin1], [-sin1, cos1]]))
        firsts.append(np.concatenate([high, high, low], axis=1))
        twists.append(np.stack(np_phase(d, np.arange(LANES), n_chan_total)))
    first = np.stack(firsts)
    twist = np.stack(twists, axis=1).astype(np.float32)
    kept = np.arange(-(kept_rows // 2), kept_rows - kept_rows // 2)
    cos2, sin2 = np_phase(kept, np.arange(LANES), LANES)
    high, low = np_split(np.block([[cos2, sin2], [-sin2, cos2]]))
    last = np.concatenate([high, high, low], axis=1)
    return first, twist, last


def delays(spectra, tables, scale, kept_rows, previous, chunk, chunks):
    n_src = len(spectra)
    count, _, rows, _ = spectra[0].shape
    outer = n_src * rows
    lane_rows = kept_rows * outer // LANES
    group = 2 if count % 2 == 0 else 1
    first, twist, last = [jnp.asarray(table) for table in tables]
    extra = [] if previous is None else [previous]
    return pl.pallas_call(
        functools.partial(delay_kernel, scale, n_src),
        grid=(1,),
        in_specs=[vmem()] * (3 + n_src) + [pl.BlockSpec(memory_space=pl.ANY)] * len(extra),
        out_specs=pl.BlockSpec((count, lane_rows, LANES), lambda i: (chunk, 0, 0)),
        out_shape=jax.ShapeDtypeStruct((chunks * count, lane_rows, LANES), f32),
        scratch_shapes=[pltpu.VMEM((group, outer, LANES), f32)] * 2,
        input_output_aliases={3 + n_src: 0} if extra else {},
        cost_estimate=cost(5),
        compiler_params=pltpu.CompilerParams(vmem_limit_bytes=VMEM_GRANT),
        name="delays",
    )(first, twist, last, *spectra, *extra)


def shards(samples, pcal_phase, tone_index, baseline_pairs):
    n_tm = lax.axis_size("tm")
    n_chan = lax.axis_size("chan")
    n_t, n_m = samples.shape[1:3]
    n_rates = n_t * n_tm
    assert n_rates == n_chan
    channels = samples.shape[5] * n_chan
    outer = channels // LANES
    kept_rows = N_DELAY // outer
    count = baseline_pairs.shape[0] // n_tm
    chunks = CHUNKS if count % CHUNKS == 0 else 1
    size = count // chunks
    me = lax.axis_index("tm")
    bound = 18.0 * n_m * n_rates
    quant = 32767.0 / bound
    scale = 1.0 / (100.0 * n_m * n_rates * channels) / (quant * quant)
    tables = delay_tables(channels, kept_rows, n_chan)

    angles = two_pi * np.outer(np.arange(n_chan), np.arange(n_rates)) / n_rates
    turns = np.vectorize(clean)(np.stack([np.cos(angles), np.sin(angles)], axis=-1))
    turn = jnp.asarray(turns.astype(np.float32))[lax.axis_index("chan")]
    levels, cal = prep(samples, tone_index, pcal_phase)
    power = None
    blocks = []
    for chunk in range(chunks):
        received = []
        for shift in range(1, n_tm):
            target = lax.rem(me + (n_tm - shift), n_tm)
            block = correlate(levels, cal, baseline_pairs, target * count + chunk * size, size)
            hops = [(j, (j - shift) % n_tm) for j in range(n_tm)]
            received.append(lax.ppermute(block, "tm", hops))
        blocks.append(received)
    for chunk in range(chunks):
        start = me * count + chunk * size
        spectra = rates(levels, cal, baseline_pairs, start, turn, blocks[chunk], quant)
        gathered = [spectra[0]]
        for shift in range(1, n_chan):
            hops = [(j, (j + shift) % n_chan) for j in range(n_chan)]
            gathered.append(lax.ppermute(spectra[shift], "chan", hops))
        power = delays(gathered, tables, scale, kept_rows, power, chunk, chunks)
    return power.reshape(1, 1, count, N_DELAY)


def solution(mesh):
    placed = (
        P("pol", ("scan", "tm"), None, None, None, "chan"),
        P("pol", None, None),
        P("chan"),
        P(),
    )
    return jax.shard_map(
        shards,
        mesh=mesh,
        in_specs=placed,
        out_specs=P("pol", ("scan", "chan"), "tm", None),
        check_vma=False,
    )
```

```python
import functools
import math

import jax
import jax.numpy as jnp
import numpy as np
from jax import lax
from jax.experimental import pallas as pl
from jax.experimental.pallas import tpu as pltpu
from jax.sharding import PartitionSpec as P


LANES = 128
NTONE = 128
N_DELAY = 8192
COST_SCALE = 2.0e6
VMEM_GRANT = 12 * 2**20
PREP_GRANT = 48 * 2**20
PREP_WIDTH = 2048
PAD = 1
two_pi = 2.0 * math.pi
bf16 = jnp.bfloat16
f32 = jnp.float32


def split_bf16(values):
    high = values.astype(bf16)
    return high, (values - high.astype(f32)).astype(bf16)


def np_split(values):
    values = np.asarray(values, np.float32)
    high = values.astype(bf16)
    return high, (values - high.astype(np.float32)).astype(bf16)


def np_phase(left, right, modulus):
    product = np.outer(left, right).astype(np.int64) % modulus
    angles = two_pi * product / modulus
    return np.cos(angles), np.sin(angles)


def prep_kernel(samples_ref, tone_ref, phase_ref, lev_ref, cal_ref, scratch):
    _, n_t, n_m, _, n_s, width = samples_ref.shape
    rows = width // LANES
    pitch = scratch.shape[0] // n_s

    def regroup(block):
        for row in range(rows):
            scratch[pl.ds(row, n_s, stride=pitch), :] = block[:, row * LANES : (row + 1) * LANES]
        return [scratch[s * pitch : s * pitch + rows, :] for s in range(n_s)]

    for t in range(n_t):
        for m in range(n_m):
            for p in range(2):
                level = (2 * samples_ref[0, t, m, p] - 3).astype(f32)
                for s, value in enumerate(regroup(level)):
                    lev_ref[t, m, p, s] = value.astype(bf16)
    slots = lax.broadcasted_iota(jnp.int32, (NTONE, width), 0)
    hot = jnp.where(slots == tone_ref[...], 1.0, 0.0).astype(bf16)
    for p, table in enumerate((jnp.cos(phase_ref[0]), jnp.sin(phase_ref[0]))):
        high, _ = split_bf16(table)
        middle, low = split_bf16(table - high.astype(f32))
        parts = jnp.concatenate([high, middle, low], axis=0)
        picked = jnp.dot(parts, hot, preferred_element_type=f32)
        total = (picked[:n_s] + picked[n_s : 2 * n_s]) + picked[2 * n_s :]
        for s, value in enumerate(regroup(total)):
            cal_ref[p, s] = value


def prep(samples, tone_index, pcal_phase):
    _, n_t, n_m, _, n_s, n_c = samples.shape
    width = min(n_c, PREP_WIDTH)
    rows = width // LANES
    return pl.pallas_call(
        prep_kernel,
        grid=(n_c // width,),
        in_specs=[
            pl.BlockSpec((1, n_t, n_m, 2, n_s, width), lambda i: (0, 0, 0, 0, 0, i)),
            pl.BlockSpec((1, width), lambda i: (0, i)),
            pl.BlockSpec((1, n_s, NTONE), lambda i: (0, 0, 0)),
        ],
        out_specs=[
            pl.BlockSpec((n_t, n_m, 2, n_s, rows, LANES), lambda i: (0, 0, 0, 0, i, 0)),
            pl.BlockSpec((2, n_s, rows, LANES), lambda i: (0, 0, i, 0)),
        ],
        out_shape=[
            jax.ShapeDtypeStruct((n_t, n_m, 2, n_s, n_c // LANES, LANES), bf16),
            jax.ShapeDtypeStruct((2, n_s, n_c // LANES, LANES), f32),
        ],
        scratch_shapes=[pltpu.VMEM((n_s * (rows + PAD), LANES), f32)],
        compiler_params=pltpu.CompilerParams(vmem_limit_bytes=PREP_GRANT),
        name="prep",
    )(samples, tone_index[None, :], pcal_phase)


def visibility_rows(lev_ref, cal_ref, first, second, rows):
    n_t, n_m = lev_ref.shape[:2]
    cos_a, sin_a = cal_ref[0, first, rows], cal_ref[1, first, rows]
    cos_e, sin_e = cal_ref[0, second, rows], cal_ref[1, second, rows]
    cos_diff = cos_a * cos_e + sin_a * sin_e
    sin_diff = sin_a * cos_e - cos_a * sin_e
    result = []
    for t in range(n_t):
        real, imag = None, None
        for m in range(n_m):
            ar, ai = lev_ref[t, m, 0, first, rows], lev_ref[t, m, 1, first, rows]
            er, ei = lev_ref[t, m, 0, second, rows], lev_ref[t, m, 1, second, rows]
            re = ar * er + ai * ei
            im = ai * er - ar * ei
            real = re if real is None else real + re
            imag = im if imag is None else imag + im
        real, imag = real.astype(f32), imag.astype(f32)
        vis_real = real * cos_diff + imag * sin_diff
        vis_imag = imag * cos_diff - real * sin_diff
        result.append((vis_real.astype(bf16), vis_imag.astype(bf16)))
    return result


def vmem():
    return pl.BlockSpec(memory_space=pltpu.VMEM)


def smem():
    return pl.BlockSpec(memory_space=pltpu.SMEM)


def cost(micros):
    return pl.CostEstimate(flops=0, bytes_accessed=int(micros * COST_SCALE), transcendentals=0)


def corr_kernel(offset, count, shift, n_tm, me_ref, pairs_ref, lev_ref, cal_ref, out_ref):
    n_rows = lev_ref.shape[4]
    step = min(16, n_rows)
    start = lax.rem(me_ref[0] + (n_tm - shift), n_tm) * count + offset

    def body(index, carry):
        first, second = pairs_ref[0, start + index], pairs_ref[1, start + index]
        for base in range(0, n_rows, step):
            rows = slice(base, base + step)
            for t, (real, imag) in enumerate(
                visibility_rows(lev_ref, cal_ref, first, second, rows)
            ):
                out_ref[index, t, 0, rows] = real
                out_ref[index, t, 1, rows] = imag
        return carry

    lax.fori_loop(0, out_ref.shape[0], body, 0)


def kernel_params():
    return pltpu.CompilerParams(vmem_limit_bytes=VMEM_GRANT)


def correlate(common, offset, size, shift):
    count, n_tm = common["count"], common["n_tm"]
    levels = common["levels"]
    shape = (size, levels.shape[0], 2) + levels.shape[4:]
    return pl.pallas_call(
        functools.partial(corr_kernel, offset, count, shift, n_tm),
        in_specs=[smem(), smem(), vmem(), vmem()],
        out_specs=vmem(),
        out_shape=jax.ShapeDtypeStruct(shape, bf16),
        cost_estimate=cost(3),
        compiler_params=kernel_params(),
        name="correlate",
    )(common["me"], common["pairs"], levels, common["cal"])


def weighted(terms):
    total = None
    for weight, value in terms:
        if weight == 0.0:
            continue
        value = value if abs(weight) == 1.0 else abs(weight) * value
        if total is None:
            total = value if weight > 0 else -value
        else:
            total = total + value if weight > 0 else total - value
    return total


def clean(value):
    rounded = round(value)
    return float(rounded) if abs(value - rounded) < 1e-12 else float(value)


def rate_kernel(quant, offset, count, spread, *refs):
    me_ref, chan_ref, pairs_ref, turn_ref, slot_ref, lev_ref, cal_ref = refs[:7]
    n_rates = turn_ref.shape[1] // 2
    n_outs = n_rates if spread else 3
    received, outs = refs[7:-n_outs], refs[-n_outs:]
    n_rows = lev_ref.shape[4]
    step = min(16, n_rows)
    start = me_ref[0] * count + offset
    chan = chan_ref[0]

    def body(index, carry):
        first, second = pairs_ref[0, start + index], pairs_ref[1, start + index]
        for base in range(0, n_rows, step):
            rows = slice(base, base + step)
            periods = list(visibility_rows(lev_ref, cal_ref, first, second, rows))
            for ref in received:
                for t in range(ref.shape[1]):
                    periods.append((ref[index, t, 0, rows], ref[index, t, 1, rows]))
            turned = []
            for t, (real, imag) in enumerate(periods):
                real, imag = real.astype(f32), imag.astype(f32)
                if t == 0:
                    turned.append((real * quant, imag * quant))
                    continue
                cosine, sine = turn_ref[chan, 2 * t] * quant, turn_ref[chan, 2 * t + 1] * quant
                turned.append((real * cosine + imag * sine, imag * cosine - real * sine))
            for s, pair in enumerate(small_dft(turned)):
                for p, value in enumerate(pair):
                    value = jnp.round(value).astype(jnp.int32).astype(jnp.int16)
                    if spread:
                        outs[s][index, p, rows] = value
                    elif s == 0:
                        outs[0][index, p, rows] = value
                    else:
                        outs[1][slot_ref[chan, s], index, p, rows] = value
        if not spread:
            outs[2][index] = outs[1][0, index]
        return carry

    lax.fori_loop(0, outs[0].shape[0], body, 0)


def small_dft(values):
    count = len(values)
    if count % 2 == 0:
        even, odd = small_dft(values[0::2]), small_dft(values[1::2])
        result = [None] * count
        for k in range(count // 2):
            angle = two_pi * k / count
            cosine, sine = clean(math.cos(angle)), clean(math.sin(angle))
            (er, ei), (odd_r, odd_i) = even[k], odd[k]
            tr = weighted([(cosine, odd_r), (sine, odd_i)])
            ti = weighted([(cosine, odd_i), (-sine, odd_r)])
            result[k] = (er + tr, ei + ti)
            result[k + count // 2] = (er - tr, ei - ti)
        return result
    result = []
    for k in range(count):
        real_terms, imag_terms = [], []
        for t, (real, imag) in enumerate(values):
            angle = two_pi * ((k * t) % count) / count
            cosine, sine = clean(math.cos(angle)), clean(math.sin(angle))
            real_terms += [(cosine, real), (sine, imag)]
            imag_terms += [(cosine, imag), (-sine, real)]
        result.append((weighted(real_terms), weighted(imag_terms)))
    return result


def rates(common, offset, size, received, spread):
    levels = common["levels"]
    shape = (size, 2) + levels.shape[4:]
    n_rates = common["n_chan"]
    shapes = [shape] * n_rates if spread else [shape, (n_rates - 1,) + shape, shape]
    return pl.pallas_call(
        functools.partial(rate_kernel, common["quant"], offset, common["count"], spread),
        in_specs=[smem()] * 5 + [vmem()] * (2 + len(received)),
        out_specs=[vmem()] * len(shapes),
        out_shape=[jax.ShapeDtypeStruct(each, jnp.int16) for each in shapes],
        cost_estimate=cost(4),
        compiler_params=kernel_params(),
        name="rates",
    )(
        common["me"],
        common["chan"],
        common["pairs"],
        common["turns"],
        common["slots"],
        levels,
        common["cal"],
        *received,
    )


def load_pair(ref, index, group):
    return [
        jnp.concatenate(
            [ref[index + g, p].astype(jnp.int32).astype(f32) for g in range(group)], axis=1
        )
        for p in range(2)
    ]


def transform(mixed, first_ref, twist_ref, last_ref, real_scratch, imag_scratch):
    group = real_scratch.shape[0]
    n_src = len(mixed)
    rows = mixed[0][0].shape[0]
    for low_digit, (real, imag) in enumerate(mixed):
        real_parts, imag_parts = split_bf16(real), split_bf16(imag)
        stacked = jnp.concatenate(
            [real_parts[0], imag_parts[0], real_parts[1], imag_parts[1]], axis=0
        )
        both = jnp.dot(first_ref[low_digit], stacked, preferred_element_type=f32)
        section = both[: 2 * rows] + both[2 * rows :]
        twist_cos, twist_sin = twist_ref[0, low_digit], twist_ref[1, low_digit]
        for g in range(group):
            real = section[:rows, g * LANES : (g + 1) * LANES]
            imag = section[rows:, g * LANES : (g + 1) * LANES]
            place = pl.ds(low_digit, rows, stride=n_src)
            real_scratch[g, place, :] = real * twist_cos + imag * twist_sin
            imag_scratch[g, place, :] = imag * twist_cos - real * twist_sin
    kept = last_ref.shape[0] // 4
    results = []
    for g in range(group):
        operand = jnp.concatenate(
            [real_scratch[g].astype(bf16), imag_scratch[g].astype(bf16)], axis=1
        )
        both = lax.dot_general(
            last_ref[...], operand, (((1,), (1,)), ((), ())), preferred_element_type=f32
        )
        final = both[: 2 * kept] + both[2 * kept :]
        results.append((final[:kept], final[kept:]))
    return results


def put_power(staged, index, real, imag, scale):
    power = (real * real + imag * imag) * scale
    kept, outer = power.shape
    halves = outer // LANES
    for half in range(halves):
        place = pl.ds(half, kept, stride=halves)
        staged[index, place, :] = power[:, half * LANES : (half + 1) * LANES]


def delay_kernel(scale, offset, n_src, first_ref, twist_ref, last_ref, *refs):
    specs = refs[:n_src]
    out_ref, real_scratch, imag_scratch, staged, sem = refs[-5:]
    total = specs[0].shape[0]
    group = real_scratch.shape[0]

    def body(step, carry):
        sources = [tuple(load_pair(spec, step * group, group)) for spec in specs]
        mixed = small_dft([sources[0]] + sources[:0:-1])
        results = transform(mixed, first_ref, twist_ref, last_ref, real_scratch, imag_scratch)
        for g, (real, imag) in enumerate(results):
            put_power(staged, step * group + g, real, imag, scale)
        return carry

    lax.fori_loop(0, total // group, body, 0)
    copy = pltpu.make_async_copy(staged, out_ref.at[pl.ds(offset, total)], sem)
    copy.start()
    copy.wait()


def mix_two(own, mate, sign):
    (own_r, own_i), (mate_r, mate_i) = own, mate
    turn_r, turn_i = mate_i * sign, -(mate_r * sign)
    return [
        (own_r + mate_r, own_i + mate_i),
        (own_r + turn_r, own_i + turn_i),
        (own_r - mate_r, own_i - mate_i),
        (own_r - turn_r, own_i - turn_i),
    ]


def chan_sign(chan_ref):
    return (1 - 2 * lax.rem(chan_ref[0], 2)).astype(f32)


def part_kernel(chan_ref, first_ref, twist_ref, last_ref, own_ref, mate_ref, *refs):
    outs, real_scratch, imag_scratch = refs[:2], refs[2], refs[3]
    group = real_scratch.shape[0]
    kept = last_ref.shape[0] // 4
    sign = chan_sign(chan_ref)

    def body(step, carry):
        for far in range(2):
            own = load_pair(own_ref.at[far + 1], step * group, group)
            mate = load_pair(mate_ref.at[far + 1], step * group, group)
            mixed = mix_two(own, mate, sign)
            results = transform(mixed, first_ref, twist_ref, last_ref, real_scratch, imag_scratch)
            for g, (real, imag) in enumerate(results):
                outs[far][step * group + g, :kept] = real.astype(bf16)
                outs[far][step * group + g, kept:] = imag.astype(bf16)
        return carry

    lax.fori_loop(0, own_ref.shape[1] // group, body, 0)


def final_kernel(scale, offset, chan_ref, join_ref, first_ref, twist_ref, last_ref, *refs):
    own_ref, mate_ref, three_ref, near_ref, far_ref = refs[:5]
    out_ref, real_scratch, imag_scratch, staged, sem = refs[-5:]
    total = own_ref.shape[0]
    group = real_scratch.shape[0]
    kept = last_ref.shape[0] // 4
    sign = chan_sign(chan_ref)
    join_r, join_i = join_ref[chan_ref[0], 0], join_ref[chan_ref[0], 1]

    def body(step, carry):
        own = load_pair(own_ref, step * group, group)
        one = load_pair(mate_ref, step * group, group)
        two = load_pair(three_ref.at[0], step * group, group)
        mate = [one[p] + two[p] for p in range(2)]
        mixed = mix_two(own, mate, sign)
        results = transform(mixed, first_ref, twist_ref, last_ref, real_scratch, imag_scratch)
        for g, (real, imag) in enumerate(results):
            index = step * group + g
            other = near_ref[index].astype(f32) + far_ref[index].astype(f32)
            other_r, other_i = other[:kept], other[kept:]
            real = real + (other_r * join_r - other_i * join_i)
            imag = imag + (other_r * join_i + other_i * join_r)
            put_power(staged, index, real, imag, scale)
        return carry

    lax.fori_loop(0, total // group, body, 0)
    copy = pltpu.make_async_copy(staged, out_ref.at[pl.ds(offset, total)], sem)
    copy.start()
    copy.wait()


def delay_tables(channels, kept_rows, n_src):
    outer = channels // LANES
    local = outer // n_src
    firsts, twists = [], []
    for low_digit in range(n_src):
        d = n_src * np.arange(local) + low_digit
        cos1, sin1 = np_phase(d, np.arange(local), outer)
        high, low = np_split(np.block([[cos1, sin1], [-sin1, cos1]]))
        firsts.append(np.block([[high, high], [low, np.zeros_like(low)]]))
        twists.append(np.stack(np_phase(d, np.arange(LANES), channels)))
    first = np.stack(firsts)
    twist = np.stack(twists, axis=1).astype(np.float32)
    kept = np.arange(-(kept_rows // 2), kept_rows - kept_rows // 2)
    cos2, sin2 = np_phase(kept, np.arange(LANES), LANES)
    high, low = np_split(np.block([[cos2, sin2], [-sin2, cos2]]))
    last = np.concatenate([high, low], axis=0)
    return tuple(jnp.asarray(table) for table in (first, twist, last))


def join_table(outer):
    d = np.arange(outer)
    angle = np.stack([2 * d, -d, d, 2 * d])[:, None, None, :] * (math.pi / 2)
    return jnp.asarray(np.round(np.concatenate([np.cos(angle), np.sin(angle)], axis=1)).astype(np.float32))


def group_of(size):
    return 2 if size % 2 == 0 else 1


def transform_scratch(common, size):
    return [pltpu.VMEM((group_of(size), common["outer"], LANES), f32)] * 2


def powers(common, kernel, scalars, operands, previous, size):
    lane_rows = common["kept"] * common["outer"] // LANES
    arrays = list(common["tables"]) + list(operands)
    extra = [] if previous is None else [previous]
    return pl.pallas_call(
        kernel,
        in_specs=[smem()] * len(scalars)
        + [vmem()] * len(arrays)
        + [pl.BlockSpec(memory_space=pl.ANY)] * len(extra),
        out_specs=pl.BlockSpec(memory_space=pl.ANY),
        out_shape=jax.ShapeDtypeStruct((common["count"], lane_rows, LANES), f32),
        scratch_shapes=transform_scratch(common, size)
        + [pltpu.VMEM((size, lane_rows, LANES), f32), pltpu.SemaphoreType.DMA(())],
        input_output_aliases={len(scalars) + len(arrays): 0} if extra else {},
        cost_estimate=cost(5),
        compiler_params=kernel_params(),
    )(*scalars, *arrays, *extra)


def partials(common, own, mate):
    size = own.shape[1]
    shape = jax.ShapeDtypeStruct((size, 2 * common["kept"], common["outer"]), bf16)
    return pl.pallas_call(
        part_kernel,
        in_specs=[smem()] + [vmem()] * 5,
        out_specs=[vmem()] * 2,
        out_shape=[shape] * 2,
        scratch_shapes=transform_scratch(common, size),
        cost_estimate=cost(8),
        compiler_params=kernel_params(),
        name="partials",
    )(common["chan"], *common["tables"], own, mate)


def plan_for(count, n_chan):
    if n_chan == 4 and count == 60:
        return PLAN, ORDER
    chunks = 5 if count % 5 == 0 else 1
    order = [f"C{i}" for i in range(min(2, chunks))]
    for i in range(chunks):
        order.append(f"R{i}")
        if i + 2 < chunks:
            order.append(f"C{i + 2}")
    return [("A", count // chunks)] * chunks, order + [f"D{i}" for i in range(chunks)]


PLAN = [("H", 6), ("A", 6), ("H", 12), ("H", 6), ("A", 12), ("A", 14), ("H", 4)]
ORDER = [
    "C0", "C1", "C4", "R0", "R1", "C3", "C2", "R4",
    "D1", "R3", "C5", "B0", "R2", "B3", "R5", "F0",
    "B2", "C6", "R6", "D4", "D5", "F3", "B6", "F2",
    "F6",
]


def shift_hops(n, shift):
    return [(j, (j + shift) % n) for j in range(n)]


def shards(samples, pcal_phase, tone_index, baseline_pairs):
    n_tm = lax.axis_size("tm")
    n_chan = lax.axis_size("chan")
    n_t, n_m = samples.shape[1:3]
    n_rates = n_t * n_tm
    assert n_rates == n_chan
    channels = samples.shape[5] * n_chan
    outer = channels // LANES
    kept_rows = N_DELAY // outer
    count = baseline_pairs.shape[0] // n_tm
    quant = 32767.0 / (18.0 * n_m * n_rates)
    scale = 1.0 / (100.0 * n_m * n_rates * channels) / (quant * quant)
    angles = two_pi * np.outer(np.arange(n_chan), np.arange(n_rates)) / n_rates
    turns = np.vectorize(clean)(np.stack([np.cos(angles), np.sin(angles)], axis=-1))
    levels, cal = prep(samples, tone_index, pcal_phase)
    common = {
        "n_tm": n_tm,
        "n_chan": n_chan,
        "count": count,
        "outer": outer,
        "kept": kept_rows,
        "quant": quant,
        "me": lax.axis_index("tm")[None],
        "chan": lax.axis_index("chan")[None],
        "pairs": baseline_pairs.T,
        "turns": jnp.asarray(turns.astype(np.float32).reshape(n_chan, 2 * n_rates)),
        "slots": jnp.asarray([[0, 0, 1, 2], [0, 1, 2, 0], [0, 0, 2, 1], [0, 2, 1, 0]], jnp.int32),
        "levels": levels,
        "cal": cal,
        "tables": delay_tables(channels, kept_rows, n_chan),
    }
    plan, order = plan_for(count, n_chan)
    offsets = [sum(size for _, size in plan[:i]) for i in range(len(plan))]
    received, held, halves = {}, {}, {}
    power = None
    for step in order:
        what, i = step[0], int(step[1:])
        (kind, size), offset = plan[i], offsets[i]
        if what == "C":
            received[i] = []
            for shift in range(1, n_tm):
                block = correlate(common, offset, size, shift)
                received[i].append(lax.ppermute(block, "tm", shift_hops(n_tm, n_tm - shift)))
        elif what == "R":
            spectra = rates(common, offset, size, received[i], kind == "A")
            if kind == "A":
                held[i] = [spectra[0]]
                for shift in range(1, n_chan):
                    hops = shift_hops(n_chan, shift)
                    held[i].append(lax.ppermute(spectra[shift], "chan", hops))
            else:
                own, three, mate = spectra
                three_in = lax.ppermute(three, "chan", [(0, 1), (3, 2)])
                mate_in = lax.ppermute(mate, "chan", [(1, 0), (2, 3)])
                held[i] = [own, mate_in, three_in]
                halves[i] = [three, three_in]
        elif what == "B":
            near, far = partials(common, *halves[i])
            held[i].append(lax.ppermute(near, "chan", [(1, 2), (2, 1)]))
            held[i].append(lax.ppermute(far, "chan", [(1, 3), (2, 0)]))
        elif what == "D":
            kernel = functools.partial(delay_kernel, scale, offset, n_chan)
            power = powers(common, kernel, [], held[i], power, size)
        else:
            kernel = functools.partial(final_kernel_of, scale, offset)
            operands = held[i] + [join_table(outer)]
            power = powers(common, kernel, [common["chan"]], operands, power, size)
    return power.reshape(1, 1, count, N_DELAY)


def final_kernel_of(scale, offset, chan_ref, first_ref, twist_ref, last_ref, *refs):
    return final_kernel(
        scale, offset, chan_ref, refs[5], first_ref, twist_ref, last_ref, *refs[:5], *refs[6:]
    )


def solution(mesh):
    placed = (
        P("pol", ("scan", "tm"), None, None, None, "chan"),
        P("pol", None, None),
        P("chan"),
        P(),
    )
    return jax.shard_map(
        shards,
        mesh=mesh,
        in_specs=placed,
        out_specs=P("pol", ("scan", "chan"), "tm", None),
        check_vma=False,
    )
```

```python
import functools
import math

import jax
import jax.numpy as jnp
import numpy as np
from jax import lax
from jax.experimental import pallas as pl
from jax.experimental.pallas import tpu as pltpu
from jax.sharding import PartitionSpec as P


LANES = 128
NTONE = 128
N_DELAY = 8192
COST_SCALE = 2.0e6
VMEM_GRANT = 12 * 2**20
PREP_GRANT = 48 * 2**20
PREP_WIDTH = 2048
PAD = 1
two_pi = 2.0 * math.pi
bf16 = jnp.bfloat16
f32 = jnp.float32


def split_bf16(values):
    high = values.astype(bf16)
    return high, (values - high.astype(f32)).astype(bf16)


def np_split(values):
    values = np.asarray(values, np.float32)
    high = values.astype(bf16)
    return high, (values - high.astype(np.float32)).astype(bf16)


def np_phase(left, right, modulus):
    product = np.outer(left, right).astype(np.int64) % modulus
    angles = two_pi * product / modulus
    return np.cos(angles), np.sin(angles)


def prep_kernel(samples_ref, tone_ref, phase_ref, lev_ref, cal_ref, scratch):
    _, n_t, n_m, _, n_s, width = samples_ref.shape
    rows = width // LANES
    pitch = scratch.shape[0] // n_s

    def regroup(block):
        for row in range(rows):
            scratch[pl.ds(row, n_s, stride=pitch), :] = block[:, row * LANES : (row + 1) * LANES]
        return [scratch[s * pitch : s * pitch + rows, :] for s in range(n_s)]

    for t in range(n_t):
        for m in range(n_m):
            for p in range(2):
                level = (2 * samples_ref[0, t, m, p] - 3).astype(f32)
                for s, value in enumerate(regroup(level)):
                    lev_ref[t, m, p, s] = value.astype(bf16)
    slots = lax.broadcasted_iota(jnp.int32, (NTONE, width), 0)
    hot = jnp.where(slots == tone_ref[...], 1.0, 0.0).astype(bf16)
    for p, table in enumerate((jnp.cos(phase_ref[0]), jnp.sin(phase_ref[0]))):
        high, _ = split_bf16(table)
        middle, low = split_bf16(table - high.astype(f32))
        parts = jnp.concatenate([high, middle, low], axis=0)
        picked = jnp.dot(parts, hot, preferred_element_type=f32)
        total = (picked[:n_s] + picked[n_s : 2 * n_s]) + picked[2 * n_s :]
        for s, value in enumerate(regroup(total)):
            cal_ref[p, s] = value


def in_hbm(array):
    return pltpu.with_memory_space_constraint(array, pltpu.HBM)


def prep(samples, tone_index, pcal_phase):
    _, n_t, n_m, _, n_s, n_c = samples.shape
    width = min(n_c, PREP_WIDTH)
    rows = width // LANES
    return pl.pallas_call(
        prep_kernel,
        grid=(n_c // width,),
        in_specs=[
            pl.BlockSpec((1, n_t, n_m, 2, n_s, width), lambda i: (0, 0, 0, 0, 0, i)),
            pl.BlockSpec((1, width), lambda i: (0, i)),
            pl.BlockSpec((1, n_s, NTONE), lambda i: (0, 0, 0)),
        ],
        out_specs=[
            pl.BlockSpec((n_t, n_m, 2, n_s, rows, LANES), lambda i: (0, 0, 0, 0, i, 0)),
            pl.BlockSpec((2, n_s, rows, LANES), lambda i: (0, 0, i, 0)),
        ],
        out_shape=[
            jax.ShapeDtypeStruct((n_t, n_m, 2, n_s, n_c // LANES, LANES), bf16),
            jax.ShapeDtypeStruct((2, n_s, n_c // LANES, LANES), f32),
        ],
        scratch_shapes=[pltpu.VMEM((n_s * (rows + PAD), LANES), f32)],
        compiler_params=pltpu.CompilerParams(vmem_limit_bytes=PREP_GRANT),
        name="prep",
    )(samples, in_hbm(tone_index[None, :]), in_hbm(pcal_phase))


def visibility_rows(lev_ref, cal_ref, first, second, rows):
    n_t, n_m = lev_ref.shape[:2]
    cos_a, sin_a = cal_ref[0, first, rows], cal_ref[1, first, rows]
    cos_e, sin_e = cal_ref[0, second, rows], cal_ref[1, second, rows]
    cos_diff = cos_a * cos_e + sin_a * sin_e
    sin_diff = sin_a * cos_e - cos_a * sin_e
    result = []
    for t in range(n_t):
        real, imag = None, None
        for m in range(n_m):
            ar, ai = lev_ref[t, m, 0, first, rows], lev_ref[t, m, 1, first, rows]
            er, ei = lev_ref[t, m, 0, second, rows], lev_ref[t, m, 1, second, rows]
            re = ar * er + ai * ei
            im = ai * er - ar * ei
            real = re if real is None else real + re
            imag = im if imag is None else imag + im
        real, imag = real.astype(f32), imag.astype(f32)
        vis_real = real * cos_diff + imag * sin_diff
        vis_imag = imag * cos_diff - real * sin_diff
        result.append((vis_real.astype(bf16), vis_imag.astype(bf16)))
    return result


def vmem():
    return pl.BlockSpec(memory_space=pltpu.VMEM)


def smem():
    return pl.BlockSpec(memory_space=pltpu.SMEM)


def cost(micros):
    return pl.CostEstimate(flops=0, bytes_accessed=int(micros * COST_SCALE), transcendentals=0)


def corr_kernel(offset, count, shifts, n_tm, me_ref, pairs_ref, lev_ref, cal_ref, *outs):
    n_rows = lev_ref.shape[4]
    step = min(16, n_rows)
    starts = [lax.rem(me_ref[0] + (n_tm - s), n_tm) * count + offset for s in shifts]

    def body(index, carry):
        for start, out_ref in zip(starts, outs):
            first, second = pairs_ref[0, start + index], pairs_ref[1, start + index]
            for base in range(0, n_rows, step):
                rows = slice(base, base + step)
                for t, (real, imag) in enumerate(
                    visibility_rows(lev_ref, cal_ref, first, second, rows)
                ):
                    out_ref[index, t, 0, rows] = real
                    out_ref[index, t, 1, rows] = imag
        return carry

    lax.fori_loop(0, outs[0].shape[0], body, 0)


def kernel_params():
    return pltpu.CompilerParams(vmem_limit_bytes=VMEM_GRANT)


def correlate(common, offset, size, shifts):
    count, n_tm = common["count"], common["n_tm"]
    levels = common["levels"]
    shape = (size, levels.shape[0], 2) + levels.shape[4:]
    return pl.pallas_call(
        functools.partial(corr_kernel, offset, count, tuple(shifts), n_tm),
        in_specs=[smem(), smem(), vmem(), vmem()],
        out_specs=[vmem()] * len(shifts),
        out_shape=[jax.ShapeDtypeStruct(shape, bf16)] * len(shifts),
        cost_estimate=cost(3),
        compiler_params=kernel_params(),
        name="correlate",
    )(common["me"], common["pairs"], levels, common["cal"])


def weighted(terms):
    total = None
    for weight, value in terms:
        if weight == 0.0:
            continue
        value = value if abs(weight) == 1.0 else abs(weight) * value
        if total is None:
            total = value if weight > 0 else -value
        else:
            total = total + value if weight > 0 else total - value
    return total


def clean(value):
    rounded = round(value)
    return float(rounded) if abs(value - rounded) < 1e-12 else float(value)


def rate_kernel(quant, spread, chan_ref, turn_ref, slot_ref, *refs):
    n_rates = turn_ref.shape[1] // 2
    n_outs = n_rates if spread else 3
    blocks, outs = refs[:-n_outs], refs[-n_outs:]
    n_rows = blocks[0].shape[3]
    step = min(16, n_rows)
    chan = chan_ref[0]

    def body(index, carry):
        for base in range(0, n_rows, step):
            rows = slice(base, base + step)
            periods = []
            for ref in blocks:
                for t in range(ref.shape[1]):
                    periods.append((ref[index, t, 0, rows], ref[index, t, 1, rows]))
            turned = []
            for t, (real, imag) in enumerate(periods):
                real, imag = real.astype(f32), imag.astype(f32)
                if t == 0:
                    turned.append((real * quant, imag * quant))
                    continue
                cosine, sine = turn_ref[chan, 2 * t] * quant, turn_ref[chan, 2 * t + 1] * quant
                turned.append((real * cosine + imag * sine, imag * cosine - real * sine))
            for s, pair in enumerate(small_dft(turned)):
                for p, value in enumerate(pair):
                    value = jnp.round(value).astype(jnp.int32).astype(jnp.int16)
                    if spread:
                        outs[s][index, p, rows] = value
                    elif s == 0:
                        outs[0][index, p, rows] = value
                    else:
                        outs[1][slot_ref[chan, s], index, p, rows] = value
        if not spread:
            outs[2][index] = outs[1][0, index]
        return carry

    lax.fori_loop(0, outs[0].shape[0], body, 0)


def small_dft(values):
    count = len(values)
    if count % 2 == 0:
        even, odd = small_dft(values[0::2]), small_dft(values[1::2])
        result = [None] * count
        for k in range(count // 2):
            angle = two_pi * k / count
            cosine, sine = clean(math.cos(angle)), clean(math.sin(angle))
            (er, ei), (odd_r, odd_i) = even[k], odd[k]
            tr = weighted([(cosine, odd_r), (sine, odd_i)])
            ti = weighted([(cosine, odd_i), (-sine, odd_r)])
            result[k] = (er + tr, ei + ti)
            result[k + count // 2] = (er - tr, ei - ti)
        return result
    result = []
    for k in range(count):
        real_terms, imag_terms = [], []
        for t, (real, imag) in enumerate(values):
            angle = two_pi * ((k * t) % count) / count
            cosine, sine = clean(math.cos(angle)), clean(math.sin(angle))
            real_terms += [(cosine, real), (sine, imag)]
            imag_terms += [(cosine, imag), (-sine, real)]
        result.append((weighted(real_terms), weighted(imag_terms)))
    return result


def rates(common, blocks, spread):
    size = blocks[0].shape[0]
    shape = (size, 2) + blocks[0].shape[3:]
    n_rates = common["n_chan"]
    shapes = [shape] * n_rates if spread else [shape, (n_rates - 1,) + shape, shape]
    return pl.pallas_call(
        functools.partial(rate_kernel, common["quant"], spread),
        in_specs=[smem()] * 3 + [vmem()] * len(blocks),
        out_specs=[vmem()] * len(shapes),
        out_shape=[jax.ShapeDtypeStruct(each, jnp.int16) for each in shapes],
        cost_estimate=cost(4),
        compiler_params=kernel_params(),
        name="rates",
    )(common["chan"], common["turns"], common["slots"], *blocks)


def load_pair(ref, index, group):
    return [
        jnp.concatenate(
            [ref[index + g, p].astype(jnp.int32).astype(f32) for g in range(group)], axis=1
        )
        for p in range(2)
    ]


def transform(mixed, first_ref, twist_ref, last_ref, real_scratch, imag_scratch):
    group = real_scratch.shape[0]
    n_src = len(mixed)
    rows = mixed[0][0].shape[0]
    for low_digit, (real, imag) in enumerate(mixed):
        real_parts, imag_parts = split_bf16(real), split_bf16(imag)
        stacked = jnp.concatenate(
            [real_parts[0], imag_parts[0], real_parts[1], imag_parts[1]], axis=0
        )
        both = jnp.dot(first_ref[low_digit], stacked, preferred_element_type=f32)
        section = both[: 2 * rows] + both[2 * rows :]
        twist_cos, twist_sin = twist_ref[0, low_digit], twist_ref[1, low_digit]
        for g in range(group):
            real = section[:rows, g * LANES : (g + 1) * LANES]
            imag = section[rows:, g * LANES : (g + 1) * LANES]
            place = pl.ds(low_digit, rows, stride=n_src)
            real_scratch[g, place, :] = real * twist_cos + imag * twist_sin
            imag_scratch[g, place, :] = imag * twist_cos - real * twist_sin
    kept = last_ref.shape[0] // 4
    results = []
    for g in range(group):
        operand = jnp.concatenate(
            [real_scratch[g].astype(bf16), imag_scratch[g].astype(bf16)], axis=1
        )
        both = lax.dot_general(
            last_ref[...], operand, (((1,), (1,)), ((), ())), preferred_element_type=f32
        )
        final = both[: 2 * kept] + both[2 * kept :]
        results.append((final[:kept], final[kept:]))
    return results


def put_power(staged, index, real, imag, scale):
    power = (real * real + imag * imag) * scale
    kept, outer = power.shape
    halves = outer // LANES
    for half in range(halves):
        place = pl.ds(half, kept, stride=halves)
        staged[index, place, :] = power[:, half * LANES : (half + 1) * LANES]


def delay_kernel(scale, offset, n_src, first_ref, twist_ref, last_ref, *refs):
    specs = refs[:n_src]
    out_ref, real_scratch, imag_scratch, staged, sem = refs[-5:]
    total = specs[0].shape[0]
    group = real_scratch.shape[0]

    def body(step, carry):
        sources = [tuple(load_pair(spec, step * group, group)) for spec in specs]
        mixed = small_dft([sources[0]] + sources[:0:-1])
        results = transform(mixed, first_ref, twist_ref, last_ref, real_scratch, imag_scratch)
        for g, (real, imag) in enumerate(results):
            put_power(staged, step * group + g, real, imag, scale)
        return carry

    lax.fori_loop(0, total // group, body, 0)
    copy = pltpu.make_async_copy(staged, out_ref.at[pl.ds(offset, total)], sem)
    copy.start()
    copy.wait()


def mix_two(own, mate, sign):
    (own_r, own_i), (mate_r, mate_i) = own, mate
    turn_r, turn_i = mate_i * sign, -(mate_r * sign)
    return [
        (own_r + mate_r, own_i + mate_i),
        (own_r + turn_r, own_i + turn_i),
        (own_r - mate_r, own_i - mate_i),
        (own_r - turn_r, own_i - turn_i),
    ]


def chan_sign(chan_ref):
    return (1 - 2 * lax.rem(chan_ref[0], 2)).astype(f32)


def part_kernel(chan_ref, first_ref, twist_ref, last_ref, own_ref, mate_ref, *refs):
    outs, real_scratch, imag_scratch = refs[:2], refs[2], refs[3]
    group = real_scratch.shape[0]
    kept = last_ref.shape[0] // 4
    sign = chan_sign(chan_ref)

    def body(step, carry):
        for far in range(2):
            own = load_pair(own_ref.at[far + 1], step * group, group)
            mate = load_pair(mate_ref.at[far + 1], step * group, group)
            mixed = mix_two(own, mate, sign)
            results = transform(mixed, first_ref, twist_ref, last_ref, real_scratch, imag_scratch)
            for g, (real, imag) in enumerate(results):
                outs[far][step * group + g, :kept] = real.astype(bf16)
                outs[far][step * group + g, kept:] = imag.astype(bf16)
        return carry

    lax.fori_loop(0, own_ref.shape[1] // group, body, 0)


def final_kernel(scale, offset, chan_ref, join_ref, first_ref, twist_ref, last_ref, *refs):
    own_ref, mate_ref, three_ref, near_ref, far_ref = refs[:5]
    out_ref, real_scratch, imag_scratch, staged, sem = refs[-5:]
    total = own_ref.shape[0]
    group = real_scratch.shape[0]
    kept = last_ref.shape[0] // 4
    sign = chan_sign(chan_ref)
    join_r, join_i = join_ref[chan_ref[0], 0], join_ref[chan_ref[0], 1]

    def body(step, carry):
        own = load_pair(own_ref, step * group, group)
        one = load_pair(mate_ref, step * group, group)
        two = load_pair(three_ref.at[0], step * group, group)
        mate = [one[p] + two[p] for p in range(2)]
        mixed = mix_two(own, mate, sign)
        results = transform(mixed, first_ref, twist_ref, last_ref, real_scratch, imag_scratch)
        for g, (real, imag) in enumerate(results):
            index = step * group + g
            other = near_ref[index].astype(f32) + far_ref[index].astype(f32)
            other_r, other_i = other[:kept], other[kept:]
            real = real + (other_r * join_r - other_i * join_i)
            imag = imag + (other_r * join_i + other_i * join_r)
            put_power(staged, index, real, imag, scale)
        return carry

    lax.fori_loop(0, total // group, body, 0)
    copy = pltpu.make_async_copy(staged, out_ref.at[pl.ds(offset, total)], sem)
    copy.start()
    copy.wait()


def delay_tables(channels, kept_rows, n_src):
    outer = channels // LANES
    local = outer // n_src
    firsts, twists = [], []
    for low_digit in range(n_src):
        d = n_src * np.arange(local) + low_digit
        cos1, sin1 = np_phase(d, np.arange(local), outer)
        high, low = np_split(np.block([[cos1, sin1], [-sin1, cos1]]))
        firsts.append(np.block([[high, high], [low, np.zeros_like(low)]]))
        twists.append(np.stack(np_phase(d, np.arange(LANES), channels)))
    first = np.stack(firsts)
    twist = np.stack(twists, axis=1).astype(np.float32)
    kept = np.arange(-(kept_rows // 2), kept_rows - kept_rows // 2)
    cos2, sin2 = np_phase(kept, np.arange(LANES), LANES)
    high, low = np_split(np.block([[cos2, sin2], [-sin2, cos2]]))
    last = np.concatenate([high, low], axis=0)
    return tuple(jnp.asarray(table) for table in (first, twist, last))


def join_table(outer):
    d = np.arange(outer)
    angle = np.stack([2 * d, -d, d, 2 * d])[:, None, None, :] * (math.pi / 2)
    return jnp.asarray(np.round(np.concatenate([np.cos(angle), np.sin(angle)], axis=1)).astype(np.float32))


def group_of(size):
    return 2 if size % 2 == 0 else 1


def transform_scratch(common, size):
    return [pltpu.VMEM((group_of(size), common["outer"], LANES), f32)] * 2


def powers(common, kernel, scalars, operands, previous, size):
    lane_rows = common["kept"] * common["outer"] // LANES
    arrays = list(common["tables"]) + list(operands)
    extra = [] if previous is None else [previous]
    return pl.pallas_call(
        kernel,
        in_specs=[smem()] * len(scalars)
        + [vmem()] * len(arrays)
        + [pl.BlockSpec(memory_space=pl.ANY)] * len(extra),
        out_specs=pl.BlockSpec(memory_space=pl.ANY),
        out_shape=jax.ShapeDtypeStruct((common["count"], lane_rows, LANES), f32),
        scratch_shapes=transform_scratch(common, size)
        + [pltpu.VMEM((size, lane_rows, LANES), f32), pltpu.SemaphoreType.DMA(())],
        input_output_aliases={len(scalars) + len(arrays): 0} if extra else {},
        cost_estimate=cost(5),
        compiler_params=kernel_params(),
    )(*scalars, *arrays, *extra)


def partials(common, own, mate):
    size = own.shape[1]
    shape = jax.ShapeDtypeStruct((size, 2 * common["kept"], common["outer"]), bf16)
    return pl.pallas_call(
        part_kernel,
        in_specs=[smem()] + [vmem()] * 5,
        out_specs=[vmem()] * 2,
        out_shape=[shape] * 2,
        scratch_shapes=transform_scratch(common, size),
        cost_estimate=cost(8),
        compiler_params=kernel_params(),
        name="partials",
    )(common["chan"], *common["tables"], own, mate)


def plan_for(count, n_chan):
    if n_chan == 4 and count == 60:
        return PLAN, ORDER
    chunks = 5 if count % 5 == 0 else 1
    order = [f"C{i}" for i in range(min(2, chunks))]
    for i in range(chunks):
        order.append(f"R{i}")
        if i + 2 < chunks:
            order.append(f"C{i + 2}")
    return [("A", count // chunks)] * chunks, order + [f"D{i}" for i in range(chunks)]


PLAN = [("A", 4), ("A", 8), ("A", 14), ("H", 10), ("A", 16), ("H", 4), ("H", 4)]
ORDER = [
    "C0", "C1", "O0", "R0", "C2", "R1", "C3", "C4",
    "C5", "R2", "R3", "R4", "D2", "B3", "C6", "D1",
    "R5", "D0", "R6", "D4", "B5", "B6", "F3", "F5",
    "F6",
]


def shift_hops(n, shift):
    return [(j, (j + shift) % n) for j in range(n)]


def shards(samples, pcal_phase, tone_index, baseline_pairs):
    n_tm = lax.axis_size("tm")
    n_chan = lax.axis_size("chan")
    n_t, n_m = samples.shape[1:3]
    n_rates = n_t * n_tm
    assert n_rates == n_chan
    channels = samples.shape[5] * n_chan
    outer = channels // LANES
    kept_rows = N_DELAY // outer
    count = baseline_pairs.shape[0] // n_tm
    quant = 32767.0 / (18.0 * n_m * n_rates)
    scale = 1.0 / (100.0 * n_m * n_rates * channels) / (quant * quant)
    angles = two_pi * np.outer(np.arange(n_chan), np.arange(n_rates)) / n_rates
    turns = np.vectorize(clean)(np.stack([np.cos(angles), np.sin(angles)], axis=-1))
    levels, cal = prep(samples, tone_index, pcal_phase)
    common = {
        "n_tm": n_tm,
        "n_chan": n_chan,
        "count": count,
        "outer": outer,
        "kept": kept_rows,
        "quant": quant,
        "me": lax.axis_index("tm")[None],
        "chan": lax.axis_index("chan")[None],
        "pairs": baseline_pairs.T,
        "turns": jnp.asarray(turns.astype(np.float32).reshape(n_chan, 2 * n_rates)),
        "slots": jnp.asarray([[0, 0, 1, 2], [0, 1, 2, 0], [0, 0, 2, 1], [0, 2, 1, 0]], jnp.int32),
        "levels": levels,
        "cal": cal,
        "tables": delay_tables(channels, kept_rows, n_chan),
    }
    plan, order = plan_for(count, n_chan)
    offsets = [sum(size for _, size in plan[:i]) for i in range(len(plan))]
    received, own_vis, held, halves = {}, {}, {}, {}
    power = None
    for step in order:
        what, i = step[0], int(step[1:])
        (kind, size), offset = plan[i], offsets[i]
        if what == "C":
            shifts = list(range(1, n_tm)) + ([0] if f"O{i}" not in order else [])
            sent = correlate(common, offset, size, shifts)
            own_vis[i] = sent[n_tm - 1 :]
            received[i] = []
            for shift in range(1, n_tm):
                hops = shift_hops(n_tm, n_tm - shift)
                received[i].append(lax.ppermute(sent[shift - 1], "tm", hops))
        elif what == "O":
            own_vis[i] = correlate(common, offset, size, [0])
        elif what == "R":
            spectra = rates(common, list(own_vis[i]) + received[i], kind == "A")
            if kind == "A":
                held[i] = [spectra[0]]
                for shift in range(1, n_chan):
                    hops = shift_hops(n_chan, shift)
                    held[i].append(lax.ppermute(spectra[shift], "chan", hops))
            else:
                own, three, mate = spectra
                three_in = lax.ppermute(three, "chan", [(0, 1), (3, 2)])
                mate_in = lax.ppermute(mate, "chan", [(1, 0), (2, 3)])
                held[i] = [own, mate_in, three_in]
                halves[i] = [three, three_in]
        elif what == "B":
            near, far = partials(common, *halves[i])
            held[i].append(lax.ppermute(near, "chan", [(1, 2), (2, 1)]))
            held[i].append(lax.ppermute(far, "chan", [(1, 3), (2, 0)]))
        elif what == "D":
            kernel = functools.partial(delay_kernel, scale, offset, n_chan)
            power = powers(common, kernel, [], held[i], power, size)
        else:
            kernel = functools.partial(final_kernel_of, scale, offset)
            operands = held[i] + [join_table(outer)]
            power = powers(common, kernel, [common["chan"]], operands, power, size)
    return power.reshape(1, 1, count, N_DELAY)


def final_kernel_of(scale, offset, chan_ref, first_ref, twist_ref, last_ref, *refs):
    return final_kernel(
        scale, offset, chan_ref, refs[5], first_ref, twist_ref, last_ref, *refs[:5], *refs[6:]
    )


def solution(mesh):
    placed = (
        P("pol", ("scan", "tm"), None, None, None, "chan"),
        P("pol", None, None),
        P("chan"),
        P(),
    )
    return jax.shard_map(
        shards,
        mesh=mesh,
        in_specs=placed,
        out_specs=P("pol", ("scan", "chan"), "tm", None),
        check_vma=False,
    )
```

```python
import functools
import math

import jax
import jax.numpy as jnp
import numpy as np
from jax import lax
from jax.experimental import pallas as pl
from jax.experimental.pallas import tpu as pltpu
from jax.sharding import PartitionSpec as P


LANES = 128
NTONE = 128
N_DELAY = 8192
COST_SCALE = 2.0e6
VMEM_GRANT = 12 * 2**20
PREP_GRANT = 48 * 2**20
PREP_WIDTH = 2048
PAD = 1
two_pi = 2.0 * math.pi
bf16 = jnp.bfloat16
f32 = jnp.float32


def split_bf16(values):
    high = values.astype(bf16)
    return high, (values - high.astype(f32)).astype(bf16)


def np_split(values):
    values = np.asarray(values, np.float32)
    high = values.astype(bf16)
    return high, (values - high.astype(np.float32)).astype(bf16)


def np_phase(left, right, modulus):
    product = np.outer(left, right).astype(np.int64) % modulus
    angles = two_pi * product / modulus
    return np.cos(angles), np.sin(angles)


def prep_kernel(samples_ref, tone_ref, phase_ref, lev_ref, cal_ref, scratch):
    _, n_t, n_m, _, n_s, width = samples_ref.shape
    rows = width // LANES
    pitch = scratch.shape[0] // n_s

    def regroup(block):
        for row in range(rows):
            scratch[pl.ds(row, n_s, stride=pitch), :] = block[:, row * LANES : (row + 1) * LANES]
        return [scratch[s * pitch : s * pitch + rows, :] for s in range(n_s)]

    for t in range(n_t):
        for m in range(n_m):
            for p in range(2):
                level = (2 * samples_ref[0, t, m, p] - 3).astype(f32)
                for s, value in enumerate(regroup(level)):
                    lev_ref[t, m, p, s] = value.astype(bf16)
    slots = lax.broadcasted_iota(jnp.int32, (NTONE, width), 0)
    hot = jnp.where(slots == tone_ref[...], 1.0, 0.0).astype(bf16)
    for p, table in enumerate((jnp.cos(phase_ref[0]), jnp.sin(phase_ref[0]))):
        high, _ = split_bf16(table)
        middle, low = split_bf16(table - high.astype(f32))
        parts = jnp.concatenate([high, middle, low], axis=0)
        picked = jnp.dot(parts, hot, preferred_element_type=f32)
        total = (picked[:n_s] + picked[n_s : 2 * n_s]) + picked[2 * n_s :]
        for s, value in enumerate(regroup(total)):
            cal_ref[p, s] = value


def in_hbm(array):
    return pltpu.with_memory_space_constraint(array, pltpu.HBM)


def prep(samples, tone_index, pcal_phase):
    _, n_t, n_m, _, n_s, n_c = samples.shape
    width = min(n_c, PREP_WIDTH)
    rows = width // LANES
    return pl.pallas_call(
        prep_kernel,
        grid=(n_c // width,),
        in_specs=[
            pl.BlockSpec((1, n_t, n_m, 2, n_s, width), lambda i: (0, 0, 0, 0, 0, i)),
            pl.BlockSpec((1, width), lambda i: (0, i)),
            pl.BlockSpec((1, n_s, NTONE), lambda i: (0, 0, 0)),
        ],
        out_specs=[
            pl.BlockSpec((n_t, n_m, 2, n_s, rows, LANES), lambda i: (0, 0, 0, 0, i, 0)),
            pl.BlockSpec((2, n_s, rows, LANES), lambda i: (0, 0, i, 0)),
        ],
        out_shape=[
            jax.ShapeDtypeStruct((n_t, n_m, 2, n_s, n_c // LANES, LANES), bf16),
            jax.ShapeDtypeStruct((2, n_s, n_c // LANES, LANES), f32),
        ],
        scratch_shapes=[pltpu.VMEM((n_s * (rows + PAD), LANES), f32)],
        compiler_params=pltpu.CompilerParams(vmem_limit_bytes=PREP_GRANT),
        name="prep",
    )(samples, in_hbm(tone_index[None, :]), in_hbm(pcal_phase))


def visibility_rows(lev_ref, cal_ref, first, second, rows):
    n_t, n_m = lev_ref.shape[:2]
    cos_a, sin_a = cal_ref[0, first, rows], cal_ref[1, first, rows]
    cos_e, sin_e = cal_ref[0, second, rows], cal_ref[1, second, rows]
    cos_diff = cos_a * cos_e + sin_a * sin_e
    sin_diff = sin_a * cos_e - cos_a * sin_e
    result = []
    for t in range(n_t):
        real, imag = None, None
        for m in range(n_m):
            ar, ai = lev_ref[t, m, 0, first, rows], lev_ref[t, m, 1, first, rows]
            er, ei = lev_ref[t, m, 0, second, rows], lev_ref[t, m, 1, second, rows]
            re = ar * er + ai * ei
            im = ai * er - ar * ei
            real = re if real is None else real + re
            imag = im if imag is None else imag + im
        real, imag = real.astype(f32), imag.astype(f32)
        vis_real = real * cos_diff + imag * sin_diff
        vis_imag = imag * cos_diff - real * sin_diff
        result.append((vis_real.astype(bf16), vis_imag.astype(bf16)))
    return result


def vmem():
    return pl.BlockSpec(memory_space=pltpu.VMEM)


def smem():
    return pl.BlockSpec(memory_space=pltpu.SMEM)


def cost(micros):
    return pl.CostEstimate(flops=0, bytes_accessed=int(micros * COST_SCALE), transcendentals=0)


def corr_kernel(offset, count, shifts, n_tm, me_ref, pairs_ref, lev_ref, cal_ref, *outs):
    n_rows = lev_ref.shape[4]
    step = min(16, n_rows)
    starts = [lax.rem(me_ref[0] + (n_tm - s), n_tm) * count + offset for s in shifts]

    def body(index, carry):
        for start, out_ref in zip(starts, outs):
            first, second = pairs_ref[0, start + index], pairs_ref[1, start + index]
            for base in range(0, n_rows, step):
                rows = slice(base, base + step)
                for t, (real, imag) in enumerate(
                    visibility_rows(lev_ref, cal_ref, first, second, rows)
                ):
                    out_ref[index, t, 0, rows] = real
                    out_ref[index, t, 1, rows] = imag
        return carry

    lax.fori_loop(0, outs[0].shape[0], body, 0)


def kernel_params():
    return pltpu.CompilerParams(vmem_limit_bytes=VMEM_GRANT)


def correlate(common, offset, size, shifts):
    count, n_tm = common["count"], common["n_tm"]
    levels = common["levels"]
    shape = (size, levels.shape[0], 2) + levels.shape[4:]
    return pl.pallas_call(
        functools.partial(corr_kernel, offset, count, tuple(shifts), n_tm),
        in_specs=[smem(), smem(), vmem(), vmem()],
        out_specs=[vmem()] * len(shifts),
        out_shape=[jax.ShapeDtypeStruct(shape, bf16)] * len(shifts),
        cost_estimate=cost(3),
        compiler_params=kernel_params(),
        name="correlate",
    )(common["me"], common["pairs"], levels, common["cal"])


def weighted(terms):
    total = None
    for weight, value in terms:
        if weight == 0.0:
            continue
        value = value if abs(weight) == 1.0 else abs(weight) * value
        if total is None:
            total = value if weight > 0 else -value
        else:
            total = total + value if weight > 0 else total - value
    return total


def clean(value):
    rounded = round(value)
    return float(rounded) if abs(value - rounded) < 1e-12 else float(value)


def rate_kernel(quant, spread, chan_ref, turn_ref, slot_ref, *refs):
    n_rates = turn_ref.shape[1] // 2
    n_outs = n_rates if spread else 3
    blocks, outs = refs[:-n_outs], refs[-n_outs:]
    n_rows = blocks[0].shape[3]
    step = min(16, n_rows)
    chan = chan_ref[0]

    def body(index, carry):
        for base in range(0, n_rows, step):
            rows = slice(base, base + step)
            periods = []
            for ref in blocks:
                for t in range(ref.shape[1]):
                    periods.append((ref[index, t, 0, rows], ref[index, t, 1, rows]))
            turned = []
            for t, (real, imag) in enumerate(periods):
                real, imag = real.astype(f32), imag.astype(f32)
                if t == 0:
                    turned.append((real * quant, imag * quant))
                    continue
                cosine, sine = turn_ref[chan, 2 * t] * quant, turn_ref[chan, 2 * t + 1] * quant
                turned.append((real * cosine + imag * sine, imag * cosine - real * sine))
            spectrum = small_dft(turned)
            for p in range(2):
                values = [jnp.round(pair[p]).astype(jnp.int32) for pair in spectrum]
                if not spread:
                    even = lax.rem(chan, 2) == 0
                    values[1], values[3] = (
                        jnp.where(even, values[1], values[3]),
                        jnp.where(even, values[3], values[1]),
                    )
                values = [value.astype(jnp.int16) for value in values]
                if spread:
                    for value, out_ref in zip(values, outs):
                        out_ref[index, p, rows] = value
                    continue
                place = slot_ref[chan]
                outs[0][index, p, rows] = values[0]
                outs[1][index, p, rows] = values[1]
                outs[2][place, index, p, rows] = values[2]
                outs[2][1 - place, index, p, rows] = values[3]
        return carry

    lax.fori_loop(0, outs[0].shape[0], body, 0)


def small_dft(values):
    count = len(values)
    if count % 2 == 0:
        even, odd = small_dft(values[0::2]), small_dft(values[1::2])
        result = [None] * count
        for k in range(count // 2):
            angle = two_pi * k / count
            cosine, sine = clean(math.cos(angle)), clean(math.sin(angle))
            (er, ei), (odd_r, odd_i) = even[k], odd[k]
            tr = weighted([(cosine, odd_r), (sine, odd_i)])
            ti = weighted([(cosine, odd_i), (-sine, odd_r)])
            result[k] = (er + tr, ei + ti)
            result[k + count // 2] = (er - tr, ei - ti)
        return result
    result = []
    for k in range(count):
        real_terms, imag_terms = [], []
        for t, (real, imag) in enumerate(values):
            angle = two_pi * ((k * t) % count) / count
            cosine, sine = clean(math.cos(angle)), clean(math.sin(angle))
            real_terms += [(cosine, real), (sine, imag)]
            imag_terms += [(cosine, imag), (-sine, real)]
        result.append((weighted(real_terms), weighted(imag_terms)))
    return result


def rates(common, blocks, spread):
    size = blocks[0].shape[0]
    shape = (size, 2) + blocks[0].shape[3:]
    n_rates = common["n_chan"]
    shapes = [shape] * n_rates if spread else [shape, shape, (2,) + shape]
    return pl.pallas_call(
        functools.partial(rate_kernel, common["quant"], spread),
        in_specs=[smem()] * 3 + [vmem()] * len(blocks),
        out_specs=[vmem()] * len(shapes),
        out_shape=[jax.ShapeDtypeStruct(each, jnp.int16) for each in shapes],
        cost_estimate=cost(4),
        compiler_params=kernel_params(),
        name="rates",
    )(common["chan"], common["turns"], common["slots"], *blocks)


def load_pair(ref, index, group):
    return [
        jnp.concatenate(
            [ref[index + g, p].astype(jnp.int32).astype(f32) for g in range(group)], axis=1
        )
        for p in range(2)
    ]


def transform(mixed, first_ref, twist_ref, last_ref, real_scratch, imag_scratch):
    group = real_scratch.shape[0]
    n_src = len(mixed)
    rows = mixed[0][0].shape[0]
    for low_digit, (real, imag) in enumerate(mixed):
        real_parts, imag_parts = split_bf16(real), split_bf16(imag)
        stacked = jnp.concatenate(
            [real_parts[0], imag_parts[0], real_parts[1], imag_parts[1]], axis=0
        )
        both = jnp.dot(first_ref[low_digit], stacked, preferred_element_type=f32)
        section = both[: 2 * rows] + both[2 * rows :]
        twist_cos, twist_sin = twist_ref[0, low_digit], twist_ref[1, low_digit]
        for g in range(group):
            real = section[:rows, g * LANES : (g + 1) * LANES]
            imag = section[rows:, g * LANES : (g + 1) * LANES]
            place = pl.ds(low_digit, rows, stride=n_src)
            real_scratch[g, place, :] = real * twist_cos + imag * twist_sin
            imag_scratch[g, place, :] = imag * twist_cos - real * twist_sin
    kept = last_ref.shape[0] // 4
    results = []
    for g in range(group):
        operand = jnp.concatenate(
            [real_scratch[g].astype(bf16), imag_scratch[g].astype(bf16)], axis=1
        )
        both = lax.dot_general(
            last_ref[...], operand, (((1,), (1,)), ((), ())), preferred_element_type=f32
        )
        final = both[: 2 * kept] + both[2 * kept :]
        results.append((final[:kept], final[kept:]))
    return results


def put_power(staged, index, real, imag, scale):
    power = (real * real + imag * imag) * scale
    kept, outer = power.shape
    halves = outer // LANES
    for half in range(halves):
        place = pl.ds(half, kept, stride=halves)
        staged[index, place, :] = power[:, half * LANES : (half + 1) * LANES]


def delay_kernel(scale, offset, n_src, first_ref, twist_ref, last_ref, *refs):
    specs = refs[:n_src]
    out_ref, real_scratch, imag_scratch, staged, sem = refs[-5:]
    total = specs[0].shape[0]
    group = real_scratch.shape[0]

    def body(step, carry):
        sources = [tuple(load_pair(spec, step * group, group)) for spec in specs]
        mixed = small_dft([sources[0]] + sources[:0:-1])
        results = transform(mixed, first_ref, twist_ref, last_ref, real_scratch, imag_scratch)
        for g, (real, imag) in enumerate(results):
            put_power(staged, step * group + g, real, imag, scale)
        return carry

    lax.fori_loop(0, total // group, body, 0)
    copy = pltpu.make_async_copy(staged, out_ref.at[pl.ds(offset, total)], sem)
    copy.start()
    copy.wait()


def mix_two(own, mate, sign):
    (own_r, own_i), (mate_r, mate_i) = own, mate
    turn_r, turn_i = mate_i * sign, -(mate_r * sign)
    return [
        (own_r + mate_r, own_i + mate_i),
        (own_r + turn_r, own_i + turn_i),
        (own_r - mate_r, own_i - mate_i),
        (own_r - turn_r, own_i - turn_i),
    ]


def chan_sign(chan_ref):
    return (1 - 2 * lax.rem(chan_ref[0], 2)).astype(f32)


def part_kernel(chan_ref, first_ref, twist_ref, last_ref, own_ref, mate_ref, *refs):
    outs, real_scratch, imag_scratch = refs[:2], refs[2], refs[3]
    group = real_scratch.shape[0]
    kept = last_ref.shape[0] // 4
    sign = chan_sign(chan_ref)

    def body(step, carry):
        for far in range(2):
            own = load_pair(own_ref.at[far], step * group, group)
            mate = load_pair(mate_ref.at[far], step * group, group)
            mixed = mix_two(own, mate, sign)
            results = transform(mixed, first_ref, twist_ref, last_ref, real_scratch, imag_scratch)
            for g, (real, imag) in enumerate(results):
                outs[far][step * group + g, :kept] = real.astype(bf16)
                outs[far][step * group + g, kept:] = imag.astype(bf16)
        return carry

    lax.fori_loop(0, own_ref.shape[1] // group, body, 0)


def final_kernel(scale, offset, chan_ref, join_ref, first_ref, twist_ref, last_ref, *refs):
    own_ref, mate_ref, near_ref, far_ref = refs[:4]
    out_ref, real_scratch, imag_scratch, staged, sem = refs[-5:]
    total = own_ref.shape[0]
    group = real_scratch.shape[0]
    kept = last_ref.shape[0] // 4
    sign = chan_sign(chan_ref)
    join_r, join_i = join_ref[chan_ref[0], 0], join_ref[chan_ref[0], 1]

    def body(step, carry):
        own = load_pair(own_ref, step * group, group)
        mate = load_pair(mate_ref, step * group, group)
        mixed = mix_two(own, mate, sign)
        results = transform(mixed, first_ref, twist_ref, last_ref, real_scratch, imag_scratch)
        for g, (real, imag) in enumerate(results):
            index = step * group + g
            other = near_ref[index].astype(f32) + far_ref[index].astype(f32)
            other_r, other_i = other[:kept], other[kept:]
            real = real + (other_r * join_r - other_i * join_i)
            imag = imag + (other_r * join_i + other_i * join_r)
            put_power(staged, index, real, imag, scale)
        return carry

    lax.fori_loop(0, total // group, body, 0)
    copy = pltpu.make_async_copy(staged, out_ref.at[pl.ds(offset, total)], sem)
    copy.start()
    copy.wait()


def delay_tables(channels, kept_rows, n_src):
    outer = channels // LANES
    local = outer // n_src
    firsts, twists = [], []
    for low_digit in range(n_src):
        d = n_src * np.arange(local) + low_digit
        cos1, sin1 = np_phase(d, np.arange(local), outer)
        high, low = np_split(np.block([[cos1, sin1], [-sin1, cos1]]))
        firsts.append(np.block([[high, high], [low, np.zeros_like(low)]]))
        twists.append(np.stack(np_phase(d, np.arange(LANES), channels)))
    first = np.stack(firsts)
    twist = np.stack(twists, axis=1).astype(np.float32)
    kept = np.arange(-(kept_rows // 2), kept_rows - kept_rows // 2)
    cos2, sin2 = np_phase(kept, np.arange(LANES), LANES)
    high, low = np_split(np.block([[cos2, sin2], [-sin2, cos2]]))
    last = np.concatenate([high, low], axis=0)
    return tuple(jnp.asarray(table) for table in (first, twist, last))


def join_table(outer):
    d = np.arange(outer)
    angle = np.stack([2 * d, -d, d, 2 * d])[:, None, None, :] * (math.pi / 2)
    return jnp.asarray(np.round(np.concatenate([np.cos(angle), np.sin(angle)], axis=1)).astype(np.float32))


def group_of(size):
    return 2 if size % 2 == 0 else 1


def transform_scratch(common, size):
    return [pltpu.VMEM((group_of(size), common["outer"], LANES), f32)] * 2


def powers(common, kernel, scalars, operands, previous, size):
    lane_rows = common["kept"] * common["outer"] // LANES
    arrays = list(common["tables"]) + list(operands)
    extra = [] if previous is None else [previous]
    return pl.pallas_call(
        kernel,
        in_specs=[smem()] * len(scalars)
        + [vmem()] * len(arrays)
        + [pl.BlockSpec(memory_space=pl.ANY)] * len(extra),
        out_specs=pl.BlockSpec(memory_space=pl.ANY),
        out_shape=jax.ShapeDtypeStruct((common["count"], lane_rows, LANES), f32),
        scratch_shapes=transform_scratch(common, size)
        + [pltpu.VMEM((size, lane_rows, LANES), f32), pltpu.SemaphoreType.DMA(())],
        input_output_aliases={len(scalars) + len(arrays): 0} if extra else {},
        cost_estimate=cost(5),
        compiler_params=kernel_params(),
    )(*scalars, *arrays, *extra)


def partials(common, own, mate):
    size = own.shape[1]
    shape = jax.ShapeDtypeStruct((size, 2 * common["kept"], common["outer"]), bf16)
    return pl.pallas_call(
        part_kernel,
        in_specs=[smem()] + [vmem()] * 5,
        out_specs=[vmem()] * 2,
        out_shape=[shape] * 2,
        scratch_shapes=transform_scratch(common, size),
        cost_estimate=cost(8),
        compiler_params=kernel_params(),
        name="partials",
    )(common["chan"], *common["tables"], own, mate)


def plan_for(count, n_chan):
    if n_chan == 4 and count == 60:
        return PLAN, ORDER
    chunks = 5 if count % 5 == 0 else 1
    order = [f"C{i}" for i in range(min(2, chunks))]
    for i in range(chunks):
        order.append(f"R{i}")
        if i + 2 < chunks:
            order.append(f"C{i + 2}")
    return [("A", count // chunks)] * chunks, order + [f"D{i}" for i in range(chunks)]


PLAN = [("A", 4), ("A", 8), ("H", 6), ("A", 12), ("H", 12), ("A", 2), ("A", 12), ("H", 4)]
ORDER = [
    "C0", "C1", "C2", "O0", "R0", "C3", "R1", "R2",
    "C4", "C5", "R3", "C6", "R4", "C7", "B2", "R5",
    "D1", "R6", "B4", "D0", "D3", "R7", "F2", "D6",
    "B7", "F4", "F7", "D5",
]


def shift_hops(n, shift):
    return [(j, (j + shift) % n) for j in range(n)]


def shards(samples, pcal_phase, tone_index, baseline_pairs):
    n_tm = lax.axis_size("tm")
    n_chan = lax.axis_size("chan")
    n_t, n_m = samples.shape[1:3]
    n_rates = n_t * n_tm
    assert n_rates == n_chan
    channels = samples.shape[5] * n_chan
    outer = channels // LANES
    kept_rows = N_DELAY // outer
    count = baseline_pairs.shape[0] // n_tm
    quant = 32767.0 / (18.0 * n_m * n_rates)
    scale = 1.0 / (100.0 * n_m * n_rates * channels) / (quant * quant)
    angles = two_pi * np.outer(np.arange(n_chan), np.arange(n_rates)) / n_rates
    turns = np.vectorize(clean)(np.stack([np.cos(angles), np.sin(angles)], axis=-1))
    levels, cal = prep(samples, tone_index, pcal_phase)
    common = {
        "n_tm": n_tm,
        "n_chan": n_chan,
        "count": count,
        "outer": outer,
        "kept": kept_rows,
        "quant": quant,
        "me": lax.axis_index("tm")[None],
        "chan": lax.axis_index("chan")[None],
        "pairs": baseline_pairs.T,
        "turns": jnp.asarray(turns.astype(np.float32).reshape(n_chan, 2 * n_rates)),
        "slots": jnp.asarray([0, 1, 1, 0], jnp.int32),
        "levels": levels,
        "cal": cal,
        "tables": delay_tables(channels, kept_rows, n_chan),
    }
    plan, order = plan_for(count, n_chan)
    offsets = [sum(size for _, size in plan[:i]) for i in range(len(plan))]
    received, own_vis, held, halves = {}, {}, {}, {}
    power = None
    for step in order:
        what, i = step[0], int(step[1:])
        (kind, size), offset = plan[i], offsets[i]
        if what == "C":
            shifts = list(range(1, n_tm)) + ([0] if f"O{i}" not in order else [])
            sent = correlate(common, offset, size, shifts)
            own_vis[i] = sent[n_tm - 1 :]
            received[i] = []
            for shift in range(1, n_tm):
                hops = shift_hops(n_tm, n_tm - shift)
                received[i].append(lax.ppermute(sent[shift - 1], "tm", hops))
        elif what == "O":
            own_vis[i] = correlate(common, offset, size, [0])
        elif what == "R":
            spectra = rates(common, list(own_vis[i]) + received[i], kind == "A")
            if kind == "A":
                held[i] = [spectra[0]]
                for shift in range(1, n_chan):
                    hops = shift_hops(n_chan, shift)
                    held[i].append(lax.ppermute(spectra[shift], "chan", hops))
            else:
                own, mate, two = spectra
                two_in = lax.ppermute(two, "chan", [(0, 1), (3, 2)])
                mate_in = lax.ppermute(mate, "chan", [(0, 1), (1, 0), (2, 3), (3, 2)])
                held[i] = [own, mate_in]
                halves[i] = [two, two_in]
        elif what == "B":
            near, far = partials(common, *halves[i])
            held[i].append(lax.ppermute(near, "chan", [(1, 2), (2, 1)]))
            held[i].append(lax.ppermute(far, "chan", [(1, 3), (2, 0)]))
        elif what == "D":
            kernel = functools.partial(delay_kernel, scale, offset, n_chan)
            power = powers(common, kernel, [], held[i], power, size)
        else:
            kernel = functools.partial(final_kernel_of, scale, offset)
            operands = held[i] + [join_table(outer)]
            power = powers(common, kernel, [common["chan"]], operands, power, size)
    return power.reshape(1, 1, count, N_DELAY)


def final_kernel_of(scale, offset, chan_ref, first_ref, twist_ref, last_ref, *refs):
    return final_kernel(
        scale, offset, chan_ref, refs[4], first_ref, twist_ref, last_ref, *refs[:4], *refs[5:]
    )


def solution(mesh):
    placed = (
        P("pol", ("scan", "tm"), None, None, None, "chan"),
        P("pol", None, None),
        P("chan"),
        P(),
    )
    return jax.shard_map(
        shards,
        mesh=mesh,
        in_specs=placed,
        out_specs=P("pol", ("scan", "chan"), "tm", None),
        check_vma=False,
    )
```

```python
import functools
import math

import jax
import jax.numpy as jnp
import numpy as np
from jax import lax
from jax.experimental import pallas as pl
from jax.experimental.pallas import tpu as pltpu
from jax.sharding import PartitionSpec as P


LANES = 128
NTONE = 128
N_DELAY = 8192
COST_SCALE = 2.0e6
VMEM_GRANT = 12 * 2**20
PREP_GRANT = 48 * 2**20
PREP_WIDTH = 2048
PAD = 1
GROUP_LIMIT = 14
two_pi = 2.0 * math.pi
bf16 = jnp.bfloat16
f32 = jnp.float32


def split_bf16(values):
    high = values.astype(bf16)
    return high, (values - high.astype(f32)).astype(bf16)


def np_split(values):
    values = np.asarray(values, np.float32)
    high = values.astype(bf16)
    return high, (values - high.astype(np.float32)).astype(bf16)


def np_phase(left, right, modulus):
    product = np.outer(left, right).astype(np.int64) % modulus
    angles = two_pi * product / modulus
    return np.cos(angles), np.sin(angles)


def prep_kernel(samples_ref, tone_ref, phase_ref, lev_ref, cal_ref, scratch):
    _, n_t, n_m, _, n_s, width = samples_ref.shape
    rows = width // LANES
    pitch = scratch.shape[0] // n_s

    def regroup(block):
        for row in range(rows):
            scratch[pl.ds(row, n_s, stride=pitch), :] = block[:, row * LANES : (row + 1) * LANES]
        return [scratch[s * pitch : s * pitch + rows, :] for s in range(n_s)]

    for t in range(n_t):
        for m in range(n_m):
            for p in range(2):
                level = (2 * samples_ref[0, t, m, p] - 3).astype(f32)
                for s, value in enumerate(regroup(level)):
                    lev_ref[t, m, p, s] = value.astype(bf16)
    slots = lax.broadcasted_iota(jnp.int32, (NTONE, width), 0)
    hot = jnp.where(slots == tone_ref[...], 1.0, 0.0).astype(bf16)
    for p, table in enumerate((jnp.cos(phase_ref[0]), jnp.sin(phase_ref[0]))):
        high, _ = split_bf16(table)
        middle, low = split_bf16(table - high.astype(f32))
        parts = jnp.concatenate([high, middle, low], axis=0)
        picked = jnp.dot(parts, hot, preferred_element_type=f32)
        total = (picked[:n_s] + picked[n_s : 2 * n_s]) + picked[2 * n_s :]
        for s, value in enumerate(regroup(total)):
            cal_ref[p, s] = value


def in_hbm(array):
    return pltpu.with_memory_space_constraint(array, pltpu.HBM)


def prep(samples, tone_index, pcal_phase):
    _, n_t, n_m, _, n_s, n_c = samples.shape
    width = min(n_c, PREP_WIDTH)
    rows = width // LANES
    return pl.pallas_call(
        prep_kernel,
        grid=(n_c // width,),
        in_specs=[
            pl.BlockSpec((1, n_t, n_m, 2, n_s, width), lambda i: (0, 0, 0, 0, 0, i)),
            pl.BlockSpec((1, width), lambda i: (0, i)),
            pl.BlockSpec((1, n_s, NTONE), lambda i: (0, 0, 0)),
        ],
        out_specs=[
            pl.BlockSpec((n_t, n_m, 2, n_s, rows, LANES), lambda i: (0, 0, 0, 0, i, 0)),
            pl.BlockSpec((2, n_s, rows, LANES), lambda i: (0, 0, i, 0)),
        ],
        out_shape=[
            jax.ShapeDtypeStruct((n_t, n_m, 2, n_s, n_c // LANES, LANES), bf16),
            jax.ShapeDtypeStruct((2, n_s, n_c // LANES, LANES), f32),
        ],
        scratch_shapes=[pltpu.VMEM((n_s * (rows + PAD), LANES), f32)],
        compiler_params=pltpu.CompilerParams(vmem_limit_bytes=PREP_GRANT),
        name="prep",
    )(samples, in_hbm(tone_index[None, :]), in_hbm(pcal_phase))


def visibility_rows(lev_ref, cal_ref, first, second, rows):
    n_t, n_m = lev_ref.shape[:2]
    cos_a, sin_a = cal_ref[0, first, rows], cal_ref[1, first, rows]
    cos_e, sin_e = cal_ref[0, second, rows], cal_ref[1, second, rows]
    cos_diff = cos_a * cos_e + sin_a * sin_e
    sin_diff = sin_a * cos_e - cos_a * sin_e
    result = []
    for t in range(n_t):
        real, imag = None, None
        for m in range(n_m):
            ar, ai = lev_ref[t, m, 0, first, rows], lev_ref[t, m, 1, first, rows]
            er, ei = lev_ref[t, m, 0, second, rows], lev_ref[t, m, 1, second, rows]
            re = ar * er + ai * ei
            im = ai * er - ar * ei
            real = re if real is None else real + re
            imag = im if imag is None else imag + im
        real, imag = real.astype(f32), imag.astype(f32)
        vis_real = real * cos_diff + imag * sin_diff
        vis_imag = imag * cos_diff - real * sin_diff
        result.append((vis_real.astype(bf16), vis_imag.astype(bf16)))
    return result


def vmem():
    return pl.BlockSpec(memory_space=pltpu.VMEM)


def smem():
    return pl.BlockSpec(memory_space=pltpu.SMEM)


def cost(micros):
    return pl.CostEstimate(flops=0, bytes_accessed=int(micros * COST_SCALE), transcendentals=0)


def corr_kernel(offset, count, shifts, n_tm, me_ref, pairs_ref, lev_ref, cal_ref, *outs):
    n_rows = lev_ref.shape[4]
    step = min(16, n_rows)
    starts = [lax.rem(me_ref[0] + (n_tm - s), n_tm) * count + offset for s in shifts]

    def body(index, carry):
        for start, out_ref in zip(starts, outs):
            first, second = pairs_ref[0, start + index], pairs_ref[1, start + index]
            for base in range(0, n_rows, step):
                rows = slice(base, base + step)
                for t, (real, imag) in enumerate(
                    visibility_rows(lev_ref, cal_ref, first, second, rows)
                ):
                    out_ref[index, t, 0, rows] = real
                    out_ref[index, t, 1, rows] = imag
        return carry

    lax.fori_loop(0, outs[0].shape[0], body, 0)


def kernel_params():
    return pltpu.CompilerParams(vmem_limit_bytes=VMEM_GRANT)


def correlate(common, offset, size, shifts):
    count, n_tm = common["count"], common["n_tm"]
    levels = common["levels"]
    shape = (size, levels.shape[0], 2) + levels.shape[4:]
    return pl.pallas_call(
        functools.partial(corr_kernel, offset, count, tuple(shifts), n_tm),
        in_specs=[smem(), smem(), vmem(), vmem()],
        out_specs=[vmem()] * len(shifts),
        out_shape=[jax.ShapeDtypeStruct(shape, bf16)] * len(shifts),
        cost_estimate=cost(3),
        compiler_params=kernel_params(),
        name="correlate",
    )(common["me"], common["pairs"], levels, common["cal"])


def weighted(terms):
    total = None
    for weight, value in terms:
        if weight == 0.0:
            continue
        value = value if abs(weight) == 1.0 else abs(weight) * value
        if total is None:
            total = value if weight > 0 else -value
        else:
            total = total + value if weight > 0 else total - value
    return total


def clean(value):
    rounded = round(value)
    return float(rounded) if abs(value - rounded) < 1e-12 else float(value)


def rate_kernel(quant, spread, chan_ref, turn_ref, slot_ref, *refs):
    n_rates = turn_ref.shape[1] // 2
    n_outs = n_rates if spread else 3
    blocks, outs = refs[:-n_outs], refs[-n_outs:]
    n_rows = blocks[0].shape[3]
    step = min(16, n_rows)
    chan = chan_ref[0]

    def body(index, carry):
        for base in range(0, n_rows, step):
            rows = slice(base, base + step)
            periods = []
            for ref in blocks:
                for t in range(ref.shape[1]):
                    periods.append((ref[index, t, 0, rows], ref[index, t, 1, rows]))
            turned = []
            for t, (real, imag) in enumerate(periods):
                real, imag = real.astype(f32), imag.astype(f32)
                if t == 0:
                    turned.append((real * quant, imag * quant))
                    continue
                cosine, sine = turn_ref[chan, 2 * t] * quant, turn_ref[chan, 2 * t + 1] * quant
                turned.append((real * cosine + imag * sine, imag * cosine - real * sine))
            spectrum = small_dft(turned)
            for p in range(2):
                values = [jnp.round(pair[p]).astype(jnp.int32) for pair in spectrum]
                if not spread:
                    even = lax.rem(chan, 2) == 0
                    values[1], values[3] = (
                        jnp.where(even, values[1], values[3]),
                        jnp.where(even, values[3], values[1]),
                    )
                values = [value.astype(jnp.int16) for value in values]
                if spread:
                    for value, out_ref in zip(values, outs):
                        out_ref[index, p, rows] = value
                    continue
                place = slot_ref[chan]
                outs[0][index, p, rows] = values[0]
                outs[1][index, p, rows] = values[1]
                outs[2][place, index, p, rows] = values[2]
                outs[2][1 - place, index, p, rows] = values[3]
        return carry

    lax.fori_loop(0, outs[0].shape[0], body, 0)


def small_dft(values):
    count = len(values)
    if count % 2 == 0:
        even, odd = small_dft(values[0::2]), small_dft(values[1::2])
        result = [None] * count
        for k in range(count // 2):
            angle = two_pi * k / count
            cosine, sine = clean(math.cos(angle)), clean(math.sin(angle))
            (er, ei), (odd_r, odd_i) = even[k], odd[k]
            tr = weighted([(cosine, odd_r), (sine, odd_i)])
            ti = weighted([(cosine, odd_i), (-sine, odd_r)])
            result[k] = (er + tr, ei + ti)
            result[k + count // 2] = (er - tr, ei - ti)
        return result
    result = []
    for k in range(count):
        real_terms, imag_terms = [], []
        for t, (real, imag) in enumerate(values):
            angle = two_pi * ((k * t) % count) / count
            cosine, sine = clean(math.cos(angle)), clean(math.sin(angle))
            real_terms += [(cosine, real), (sine, imag)]
            imag_terms += [(cosine, imag), (-sine, real)]
        result.append((weighted(real_terms), weighted(imag_terms)))
    return result


def rates(common, blocks, spread):
    size = blocks[0].shape[0]
    shape = (size, 2) + blocks[0].shape[3:]
    n_rates = common["n_chan"]
    shapes = [shape] * n_rates if spread else [shape, shape, (2,) + shape]
    return pl.pallas_call(
        functools.partial(rate_kernel, common["quant"], spread),
        in_specs=[smem()] * 3 + [vmem()] * len(blocks),
        out_specs=[vmem()] * len(shapes),
        out_shape=[jax.ShapeDtypeStruct(each, jnp.int16) for each in shapes],
        cost_estimate=cost(4),
        compiler_params=kernel_params(),
        name="rates",
    )(common["chan"], common["turns"], common["slots"], *blocks)


def load_pair(ref, index, group):
    return [
        jnp.concatenate(
            [ref[index + g, p].astype(jnp.int32).astype(f32) for g in range(group)], axis=1
        )
        for p in range(2)
    ]


def transform(mixed, first_ref, twist_ref, last_ref, real_scratch, imag_scratch):
    group = real_scratch.shape[0]
    n_src = len(mixed)
    rows = mixed[0][0].shape[0]
    for low_digit, (real, imag) in enumerate(mixed):
        real_parts, imag_parts = split_bf16(real), split_bf16(imag)
        stacked = jnp.concatenate(
            [real_parts[0], imag_parts[0], real_parts[1], imag_parts[1]], axis=0
        )
        both = jnp.dot(first_ref[low_digit], stacked, preferred_element_type=f32)
        section = both[: 2 * rows] + both[2 * rows :]
        twist_cos, twist_sin = twist_ref[0, low_digit], twist_ref[1, low_digit]
        for g in range(group):
            real = section[:rows, g * LANES : (g + 1) * LANES]
            imag = section[rows:, g * LANES : (g + 1) * LANES]
            place = pl.ds(low_digit, rows, stride=n_src)
            real_scratch[g, place, :] = real * twist_cos + imag * twist_sin
            imag_scratch[g, place, :] = imag * twist_cos - real * twist_sin
    kept = last_ref.shape[0] // 4
    results = []
    for g in range(group):
        operand = jnp.concatenate(
            [real_scratch[g].astype(bf16), imag_scratch[g].astype(bf16)], axis=1
        )
        both = lax.dot_general(
            last_ref[...], operand, (((1,), (1,)), ((), ())), preferred_element_type=f32
        )
        final = both[: 2 * kept] + both[2 * kept :]
        results.append((final[:kept], final[kept:]))
    return results


def put_power(staged, index, real, imag, scale):
    power = (real * real + imag * imag) * scale
    kept, outer = power.shape
    halves = outer // LANES
    for half in range(halves):
        place = pl.ds(half, kept, stride=halves)
        staged[index, place, :] = power[:, half * LANES : (half + 1) * LANES]


def delay_kernel(scale, offset, n_src, first_ref, twist_ref, last_ref, *refs):
    specs = refs[:n_src]
    out_ref, real_scratch, imag_scratch, staged, sem = refs[-5:]
    total = specs[0].shape[0]
    group = real_scratch.shape[0]

    def body(step, carry):
        sources = [tuple(load_pair(spec, step * group, group)) for spec in specs]
        mixed = small_dft([sources[0]] + sources[:0:-1])
        results = transform(mixed, first_ref, twist_ref, last_ref, real_scratch, imag_scratch)
        for g, (real, imag) in enumerate(results):
            put_power(staged, step * group + g, real, imag, scale)
        return carry

    lax.fori_loop(0, total // group, body, 0)
    copy = pltpu.make_async_copy(staged, out_ref.at[pl.ds(offset, total)], sem)
    copy.start()
    copy.wait()


def mix_two(own, mate, sign):
    (own_r, own_i), (mate_r, mate_i) = own, mate
    turn_r, turn_i = mate_i * sign, -(mate_r * sign)
    return [
        (own_r + mate_r, own_i + mate_i),
        (own_r + turn_r, own_i + turn_i),
        (own_r - mate_r, own_i - mate_i),
        (own_r - turn_r, own_i - turn_i),
    ]


def chan_sign(chan_ref):
    return (1 - 2 * lax.rem(chan_ref[0], 2)).astype(f32)


def part_kernel(chan_ref, first_ref, twist_ref, last_ref, own_ref, mate_ref, *refs):
    outs, real_scratch, imag_scratch = refs[:2], refs[2], refs[3]
    group = real_scratch.shape[0]
    kept = last_ref.shape[0] // 4
    sign = chan_sign(chan_ref)

    def body(step, carry):
        for far in range(2):
            own = load_pair(own_ref.at[far], step * group, group)
            mate = load_pair(mate_ref.at[far], step * group, group)
            mixed = mix_two(own, mate, sign)
            results = transform(mixed, first_ref, twist_ref, last_ref, real_scratch, imag_scratch)
            for g, (real, imag) in enumerate(results):
                outs[far][step * group + g, :kept] = real.astype(bf16)
                outs[far][step * group + g, kept:] = imag.astype(bf16)
        return carry

    lax.fori_loop(0, own_ref.shape[1] // group, body, 0)


def final_kernel(scale, offset, chan_ref, join_ref, first_ref, twist_ref, last_ref, *refs):
    own_ref, mate_ref, near_ref, far_ref = refs[:4]
    out_ref, real_scratch, imag_scratch, staged, sem = refs[-5:]
    total = own_ref.shape[0]
    group = real_scratch.shape[0]
    kept = last_ref.shape[0] // 4
    sign = chan_sign(chan_ref)
    join_r, join_i = join_ref[chan_ref[0], 0], join_ref[chan_ref[0], 1]

    def body(step, carry):
        own = load_pair(own_ref, step * group, group)
        mate = load_pair(mate_ref, step * group, group)
        mixed = mix_two(own, mate, sign)
        results = transform(mixed, first_ref, twist_ref, last_ref, real_scratch, imag_scratch)
        for g, (real, imag) in enumerate(results):
            index = step * group + g
            other = near_ref[index].astype(f32) + far_ref[index].astype(f32)
            other_r, other_i = other[:kept], other[kept:]
            real = real + (other_r * join_r - other_i * join_i)
            imag = imag + (other_r * join_i + other_i * join_r)
            put_power(staged, index, real, imag, scale)
        return carry

    lax.fori_loop(0, total // group, body, 0)
    copy = pltpu.make_async_copy(staged, out_ref.at[pl.ds(offset, total)], sem)
    copy.start()
    copy.wait()


def delay_tables(channels, kept_rows, n_src):
    outer = channels // LANES
    local = outer // n_src
    firsts, twists = [], []
    for low_digit in range(n_src):
        d = n_src * np.arange(local) + low_digit
        cos1, sin1 = np_phase(d, np.arange(local), outer)
        high, low = np_split(np.block([[cos1, sin1], [-sin1, cos1]]))
        firsts.append(np.block([[high, high], [low, np.zeros_like(low)]]))
        twists.append(np.stack(np_phase(d, np.arange(LANES), channels)))
    first = np.stack(firsts)
    twist = np.stack(twists, axis=1).astype(np.float32)
    kept = np.arange(-(kept_rows // 2), kept_rows - kept_rows // 2)
    cos2, sin2 = np_phase(kept, np.arange(LANES), LANES)
    high, low = np_split(np.block([[cos2, sin2], [-sin2, cos2]]))
    last = np.concatenate([high, low], axis=0)
    return tuple(jnp.asarray(table) for table in (first, twist, last))


def join_table(outer):
    d = np.arange(outer)
    angle = np.stack([2 * d, -d, d, 2 * d])[:, None, None, :] * (math.pi / 2)
    return jnp.asarray(np.round(np.concatenate([np.cos(angle), np.sin(angle)], axis=1)).astype(np.float32))


def group_of(size):
    return max(g for g in range(1, GROUP_LIMIT + 1) if size % g == 0)


def transform_scratch(common, size):
    return [pltpu.VMEM((group_of(size), common["outer"], LANES), f32)] * 2


def powers(common, kernel, scalars, operands, previous, size):
    lane_rows = common["kept"] * common["outer"] // LANES
    arrays = list(common["tables"]) + list(operands)
    extra = [] if previous is None else [previous]
    return pl.pallas_call(
        kernel,
        in_specs=[smem()] * len(scalars)
        + [vmem()] * len(arrays)
        + [pl.BlockSpec(memory_space=pl.ANY)] * len(extra),
        out_specs=pl.BlockSpec(memory_space=pl.ANY),
        out_shape=jax.ShapeDtypeStruct((common["count"], lane_rows, LANES), f32),
        scratch_shapes=transform_scratch(common, size)
        + [pltpu.VMEM((size, lane_rows, LANES), f32), pltpu.SemaphoreType.DMA(())],
        input_output_aliases={len(scalars) + len(arrays): 0} if extra else {},
        cost_estimate=cost(5),
        compiler_params=kernel_params(),
    )(*scalars, *arrays, *extra)


def partials(common, own, mate):
    size = own.shape[1]
    shape = jax.ShapeDtypeStruct((size, 2 * common["kept"], common["outer"]), bf16)
    return pl.pallas_call(
        part_kernel,
        in_specs=[smem()] + [vmem()] * 5,
        out_specs=[vmem()] * 2,
        out_shape=[shape] * 2,
        scratch_shapes=transform_scratch(common, size),
        cost_estimate=cost(8),
        compiler_params=kernel_params(),
        name="partials",
    )(common["chan"], *common["tables"], own, mate)


def plan_for(count, n_chan):
    if n_chan == 4 and count == 60:
        return PLAN, ORDER
    chunks = 5 if count % 5 == 0 else 1
    order = [f"C{i}" for i in range(min(2, chunks))]
    for i in range(chunks):
        order.append(f"R{i}")
        if i + 2 < chunks:
            order.append(f"C{i + 2}")
    return [("A", count // chunks)] * chunks, order + [f"D{i}" for i in range(chunks)]


PLAN = [("A", 6), ("H", 6), ("H", 8), ("H", 12), ("A", 12), ("A", 8), ("A", 4), ("H", 4)]
ORDER = [
    "C0", "C1", "O0", "C4", "R0", "R1", "C2", "C3",
    "R4", "B1", "R2", "C5", "D0", "C7", "R3", "R5",
    "C6", "B2", "F1", "R6", "R7", "B3", "D4", "D6",
    "F2", "B7", "F3", "D5", "F7",
]


def shift_hops(n, shift):
    return [(j, (j + shift) % n) for j in range(n)]


def shards(samples, pcal_phase, tone_index, baseline_pairs):
    n_tm = lax.axis_size("tm")
    n_chan = lax.axis_size("chan")
    n_t, n_m = samples.shape[1:3]
    n_rates = n_t * n_tm
    assert n_rates == n_chan
    channels = samples.shape[5] * n_chan
    outer = channels // LANES
    kept_rows = N_DELAY // outer
    count = baseline_pairs.shape[0] // n_tm
    quant = 32767.0 / (18.0 * n_m * n_rates)
    scale = 1.0 / (100.0 * n_m * n_rates * channels) / (quant * quant)
    angles = two_pi * np.outer(np.arange(n_chan), np.arange(n_rates)) / n_rates
    turns = np.vectorize(clean)(np.stack([np.cos(angles), np.sin(angles)], axis=-1))
    levels, cal = prep(samples, tone_index, pcal_phase)
    common = {
        "n_tm": n_tm,
        "n_chan": n_chan,
        "count": count,
        "outer": outer,
        "kept": kept_rows,
        "quant": quant,
        "me": lax.axis_index("tm")[None],
        "chan": lax.axis_index("chan")[None],
        "pairs": baseline_pairs.T,
        "turns": jnp.asarray(turns.astype(np.float32).reshape(n_chan, 2 * n_rates)),
        "slots": jnp.asarray([0, 1, 1, 0], jnp.int32),
        "levels": levels,
        "cal": cal,
        "tables": delay_tables(channels, kept_rows, n_chan),
    }
    plan, order = plan_for(count, n_chan)
    offsets = [sum(size for _, size in plan[:i]) for i in range(len(plan))]
    received, own_vis, held, halves = {}, {}, {}, {}
    power = None
    for step in order:
        what, i = step[0], int(step[1:])
        (kind, size), offset = plan[i], offsets[i]
        if what == "C":
            shifts = list(range(1, n_tm)) + ([0] if f"O{i}" not in order else [])
            sent = correlate(common, offset, size, shifts)
            own_vis[i] = sent[n_tm - 1 :]
            received[i] = []
            for shift in range(1, n_tm):
                hops = shift_hops(n_tm, n_tm - shift)
                received[i].append(lax.ppermute(sent[shift - 1], "tm", hops))
        elif what == "O":
            own_vis[i] = correlate(common, offset, size, [0])
        elif what == "R":
            spectra = rates(common, list(own_vis[i]) + received[i], kind == "A")
            if kind == "A":
                held[i] = [spectra[0]]
                for shift in range(1, n_chan):
                    hops = shift_hops(n_chan, shift)
                    held[i].append(lax.ppermute(spectra[shift], "chan", hops))
            else:
                own, mate, two = spectra
                two_in = lax.ppermute(two, "chan", [(0, 1), (3, 2)])
                mate_in = lax.ppermute(mate, "chan", [(0, 1), (1, 0), (2, 3), (3, 2)])
                held[i] = [own, mate_in]
                halves[i] = [two, two_in]
        elif what == "B":
            near, far = partials(common, *halves[i])
            held[i].append(lax.ppermute(near, "chan", [(1, 2), (2, 1)]))
            held[i].append(lax.ppermute(far, "chan", [(1, 3), (2, 0)]))
        elif what == "D":
            kernel = functools.partial(delay_kernel, scale, offset, n_chan)
            power = powers(common, kernel, [], held[i], power, size)
        else:
            kernel = functools.partial(final_kernel_of, scale, offset)
            operands = held[i] + [join_table(outer)]
            power = powers(common, kernel, [common["chan"]], operands, power, size)
    return power.reshape(1, 1, count, N_DELAY)


def final_kernel_of(scale, offset, chan_ref, first_ref, twist_ref, last_ref, *refs):
    return final_kernel(
        scale, offset, chan_ref, refs[4], first_ref, twist_ref, last_ref, *refs[:4], *refs[5:]
    )


def solution(mesh):
    placed = (
        P("pol", ("scan", "tm"), None, None, None, "chan"),
        P("pol", None, None),
        P("chan"),
        P(),
    )
    return jax.shard_map(
        shards,
        mesh=mesh,
        in_specs=placed,
        out_specs=P("pol", ("scan", "chan"), "tm", None),
        check_vma=False,
    )
```

```python
import functools
import math

import jax
import jax.numpy as jnp
import numpy as np
from jax import lax
from jax.experimental import pallas as pl
from jax.experimental.pallas import tpu as pltpu
from jax.sharding import PartitionSpec as P


LANES = 128
NTONE = 128
N_DELAY = 8192
COST_SCALE = 2.0e6
VMEM_GRANT = 12 * 2**20
PREP_GRANT = 48 * 2**20
PREP_WIDTH = 2048
PAD = 1
GROUP_LIMIT = 14
two_pi = 2.0 * math.pi
bf16 = jnp.bfloat16
f32 = jnp.float32


def split_bf16(values):
    high = values.astype(bf16)
    return high, (values - high.astype(f32)).astype(bf16)


def np_split(values):
    values = np.asarray(values, np.float32)
    high = values.astype(bf16)
    return high, (values - high.astype(np.float32)).astype(bf16)


def np_phase(left, right, modulus):
    product = np.outer(left, right).astype(np.int64) % modulus
    angles = two_pi * product / modulus
    return np.cos(angles), np.sin(angles)


def prep_kernel(samples_ref, tone_ref, phase_ref, lev_ref, cal_ref, scratch):
    _, n_t, n_m, _, n_s, width = samples_ref.shape
    rows = width // LANES
    pitch = scratch.shape[0] // n_s

    def regroup(block):
        for row in range(rows):
            scratch[pl.ds(row, n_s, stride=pitch), :] = block[:, row * LANES : (row + 1) * LANES]
        return [scratch[s * pitch : s * pitch + rows, :] for s in range(n_s)]

    for t in range(n_t):
        for m in range(n_m):
            for p in range(2):
                level = (2 * samples_ref[0, t, m, p] - 3).astype(f32)
                for s, value in enumerate(regroup(level)):
                    lev_ref[t, m, p, s] = value.astype(bf16)
    slots = lax.broadcasted_iota(jnp.int32, (NTONE, width), 0)
    hot = jnp.where(slots == tone_ref[...], 1.0, 0.0).astype(bf16)
    for p, table in enumerate((jnp.cos(phase_ref[0]), jnp.sin(phase_ref[0]))):
        high, _ = split_bf16(table)
        middle, low = split_bf16(table - high.astype(f32))
        parts = jnp.concatenate([high, middle, low], axis=0)
        picked = jnp.dot(parts, hot, preferred_element_type=f32)
        total = (picked[:n_s] + picked[n_s : 2 * n_s]) + picked[2 * n_s :]
        for s, value in enumerate(regroup(total)):
            cal_ref[p, s] = value


def in_hbm(array):
    return pltpu.with_memory_space_constraint(array, pltpu.HBM)


def prep(samples, tone_index, pcal_phase):
    _, n_t, n_m, _, n_s, n_c = samples.shape
    width = min(n_c, PREP_WIDTH)
    rows = width // LANES
    return pl.pallas_call(
        prep_kernel,
        grid=(n_c // width,),
        in_specs=[
            pl.BlockSpec((1, n_t, n_m, 2, n_s, width), lambda i: (0, 0, 0, 0, 0, i)),
            pl.BlockSpec((1, width), lambda i: (0, i)),
            pl.BlockSpec((1, n_s, NTONE), lambda i: (0, 0, 0)),
        ],
        out_specs=[
            pl.BlockSpec((n_t, n_m, 2, n_s, rows, LANES), lambda i: (0, 0, 0, 0, i, 0)),
            pl.BlockSpec((2, n_s, rows, LANES), lambda i: (0, 0, i, 0)),
        ],
        out_shape=[
            jax.ShapeDtypeStruct((n_t, n_m, 2, n_s, n_c // LANES, LANES), bf16),
            jax.ShapeDtypeStruct((2, n_s, n_c // LANES, LANES), f32),
        ],
        scratch_shapes=[pltpu.VMEM((n_s * (rows + PAD), LANES), f32)],
        compiler_params=pltpu.CompilerParams(vmem_limit_bytes=PREP_GRANT),
        name="prep",
    )(samples, in_hbm(tone_index[None, :]), in_hbm(pcal_phase))


def visibility_rows(lev_ref, cal_ref, first, second, rows):
    n_t, n_m = lev_ref.shape[:2]
    cos_a, sin_a = cal_ref[0, first, rows], cal_ref[1, first, rows]
    cos_e, sin_e = cal_ref[0, second, rows], cal_ref[1, second, rows]
    cos_diff = cos_a * cos_e + sin_a * sin_e
    sin_diff = sin_a * cos_e - cos_a * sin_e
    result = []
    for t in range(n_t):
        real, imag = None, None
        for m in range(n_m):
            ar, ai = lev_ref[t, m, 0, first, rows], lev_ref[t, m, 1, first, rows]
            er, ei = lev_ref[t, m, 0, second, rows], lev_ref[t, m, 1, second, rows]
            re = ar * er + ai * ei
            im = ai * er - ar * ei
            real = re if real is None else real + re
            imag = im if imag is None else imag + im
        real, imag = real.astype(f32), imag.astype(f32)
        vis_real = real * cos_diff + imag * sin_diff
        vis_imag = imag * cos_diff - real * sin_diff
        result.append((vis_real.astype(bf16), vis_imag.astype(bf16)))
    return result


def vmem():
    return pl.BlockSpec(memory_space=pltpu.VMEM)


def smem():
    return pl.BlockSpec(memory_space=pltpu.SMEM)


def cost(micros):
    return pl.CostEstimate(flops=0, bytes_accessed=int(micros * COST_SCALE), transcendentals=0)


def corr_kernel(offset, count, shifts, n_tm, me_ref, pairs_ref, lev_ref, cal_ref, *outs):
    n_rows = lev_ref.shape[4]
    step = min(16, n_rows)
    starts = [lax.rem(me_ref[0] + (n_tm - s), n_tm) * count + offset for s in shifts]

    def body(index, carry):
        for start, out_ref in zip(starts, outs):
            first, second = pairs_ref[0, start + index], pairs_ref[1, start + index]
            for base in range(0, n_rows, step):
                rows = slice(base, base + step)
                for t, (real, imag) in enumerate(
                    visibility_rows(lev_ref, cal_ref, first, second, rows)
                ):
                    out_ref[index, t, 0, rows] = real
                    out_ref[index, t, 1, rows] = imag
        return carry

    lax.fori_loop(0, outs[0].shape[0], body, 0)


def kernel_params():
    return pltpu.CompilerParams(vmem_limit_bytes=VMEM_GRANT)


def correlate(common, offset, size, shifts):
    count, n_tm = common["count"], common["n_tm"]
    levels = common["levels"]
    shape = (size, levels.shape[0], 2) + levels.shape[4:]
    return pl.pallas_call(
        functools.partial(corr_kernel, offset, count, tuple(shifts), n_tm),
        in_specs=[smem(), smem(), vmem(), vmem()],
        out_specs=[vmem()] * len(shifts),
        out_shape=[jax.ShapeDtypeStruct(shape, bf16)] * len(shifts),
        cost_estimate=cost(3),
        compiler_params=kernel_params(),
        name="correlate",
    )(common["me"], common["pairs"], levels, common["cal"])


def weighted(terms):
    total = None
    for weight, value in terms:
        if weight == 0.0:
            continue
        value = value if abs(weight) == 1.0 else abs(weight) * value
        if total is None:
            total = value if weight > 0 else -value
        else:
            total = total + value if weight > 0 else total - value
    return total


def clean(value):
    rounded = round(value)
    return float(rounded) if abs(value - rounded) < 1e-12 else float(value)


def rate_kernel(quant, spread, chan_ref, turn_ref, slot_ref, *refs):
    n_rates = turn_ref.shape[1] // 2
    n_outs = n_rates if spread else 3
    blocks, outs = refs[:-n_outs], refs[-n_outs:]
    n_rows = blocks[0].shape[3]
    step = min(16, n_rows)
    chan = chan_ref[0]

    def body(index, carry):
        for base in range(0, n_rows, step):
            rows = slice(base, base + step)
            periods = []
            for ref in blocks:
                for t in range(ref.shape[1]):
                    periods.append((ref[index, t, 0, rows], ref[index, t, 1, rows]))
            turned = []
            for t, (real, imag) in enumerate(periods):
                real, imag = real.astype(f32), imag.astype(f32)
                if t == 0:
                    turned.append((real * quant, imag * quant))
                    continue
                cosine, sine = turn_ref[chan, 2 * t] * quant, turn_ref[chan, 2 * t + 1] * quant
                turned.append((real * cosine + imag * sine, imag * cosine - real * sine))
            spectrum = small_dft(turned)
            for p in range(2):
                values = [jnp.round(pair[p]).astype(jnp.int32) for pair in spectrum]
                if not spread:
                    even = lax.rem(chan, 2) == 0
                    values[1], values[3] = (
                        jnp.where(even, values[1], values[3]),
                        jnp.where(even, values[3], values[1]),
                    )
                values = [value.astype(jnp.int16) for value in values]
                if spread:
                    for value, out_ref in zip(values, outs):
                        out_ref[index, p, rows] = value
                    continue
                place = slot_ref[chan]
                outs[0][index, p, rows] = values[0]
                outs[1][index, p, rows] = values[1]
                outs[2][place, index, p, rows] = values[2]
                outs[2][1 - place, index, p, rows] = values[3]
        return carry

    lax.fori_loop(0, outs[0].shape[0], body, 0)


def small_dft(values):
    count = len(values)
    if count % 2 == 0:
        even, odd = small_dft(values[0::2]), small_dft(values[1::2])
        result = [None] * count
        for k in range(count // 2):
            angle = two_pi * k / count
            cosine, sine = clean(math.cos(angle)), clean(math.sin(angle))
            (er, ei), (odd_r, odd_i) = even[k], odd[k]
            tr = weighted([(cosine, odd_r), (sine, odd_i)])
            ti = weighted([(cosine, odd_i), (-sine, odd_r)])
            result[k] = (er + tr, ei + ti)
            result[k + count // 2] = (er - tr, ei - ti)
        return result
    result = []
    for k in range(count):
        real_terms, imag_terms = [], []
        for t, (real, imag) in enumerate(values):
            angle = two_pi * ((k * t) % count) / count
            cosine, sine = clean(math.cos(angle)), clean(math.sin(angle))
            real_terms += [(cosine, real), (sine, imag)]
            imag_terms += [(cosine, imag), (-sine, real)]
        result.append((weighted(real_terms), weighted(imag_terms)))
    return result


def rates(common, blocks, spread):
    size = blocks[0].shape[0]
    shape = (size, 2) + blocks[0].shape[3:]
    n_rates = common["n_chan"]
    shapes = [shape] * n_rates if spread else [shape, shape, (2,) + shape]
    return pl.pallas_call(
        functools.partial(rate_kernel, common["quant"], spread),
        in_specs=[smem()] * 3 + [vmem()] * len(blocks),
        out_specs=[vmem()] * len(shapes),
        out_shape=[jax.ShapeDtypeStruct(each, jnp.int16) for each in shapes],
        cost_estimate=cost(4),
        compiler_params=kernel_params(),
        name="rates",
    )(common["chan"], common["turns"], common["slots"], *blocks)


def load_pair(ref, index, group):
    return [
        jnp.concatenate(
            [ref[index + g, p].astype(jnp.int32).astype(f32) for g in range(group)], axis=1
        )
        for p in range(2)
    ]


def transform(mixed, first_ref, twist_ref, last_ref, real_scratch, imag_scratch):
    group = real_scratch.shape[0]
    n_src = len(mixed)
    rows = mixed[0][0].shape[0]
    for low_digit, (real, imag) in enumerate(mixed):
        real_parts, imag_parts = split_bf16(real), split_bf16(imag)
        stacked = jnp.concatenate(
            [real_parts[0], imag_parts[0], real_parts[1], imag_parts[1]], axis=0
        )
        both = jnp.dot(first_ref[low_digit], stacked, preferred_element_type=f32)
        section = both[: 2 * rows] + both[2 * rows :]
        twist_cos, twist_sin = twist_ref[0, low_digit], twist_ref[1, low_digit]
        for g in range(group):
            real = section[:rows, g * LANES : (g + 1) * LANES]
            imag = section[rows:, g * LANES : (g + 1) * LANES]
            place = pl.ds(low_digit, rows, stride=n_src)
            real_scratch[g, place, :] = real * twist_cos + imag * twist_sin
            imag_scratch[g, place, :] = imag * twist_cos - real * twist_sin
    kept = last_ref.shape[0] // 4
    results = []
    for g in range(group):
        operand = jnp.concatenate(
            [real_scratch[g].astype(bf16), imag_scratch[g].astype(bf16)], axis=1
        )
        both = lax.dot_general(
            last_ref[...], operand, (((1,), (1,)), ((), ())), preferred_element_type=f32
        )
        final = both[: 2 * kept] + both[2 * kept :]
        results.append((final[:kept], final[kept:]))
    return results


def put_power(staged, index, real, imag, scale):
    power = (real * real + imag * imag) * scale
    kept, outer = power.shape
    halves = outer // LANES
    for half in range(halves):
        place = pl.ds(half, kept, stride=halves)
        staged[index, place, :] = power[:, half * LANES : (half + 1) * LANES]


def delay_kernel(scale, offset, n_src, first_ref, twist_ref, last_ref, *refs):
    specs = refs[:n_src]
    out_ref, real_scratch, imag_scratch, staged, sem = refs[-5:]
    total = specs[0].shape[0]
    group = real_scratch.shape[0]

    def body(step, carry):
        sources = [tuple(load_pair(spec, step * group, group)) for spec in specs]
        mixed = small_dft([sources[0]] + sources[:0:-1])
        results = transform(mixed, first_ref, twist_ref, last_ref, real_scratch, imag_scratch)
        for g, (real, imag) in enumerate(results):
            put_power(staged, step * group + g, real, imag, scale)
        return carry

    lax.fori_loop(0, total // group, body, 0)
    copy = pltpu.make_async_copy(staged, out_ref.at[pl.ds(offset, total)], sem)
    copy.start()
    copy.wait()


def mix_two(own, mate, sign):
    (own_r, own_i), (mate_r, mate_i) = own, mate
    turn_r, turn_i = mate_i * sign, -(mate_r * sign)
    return [
        (own_r + mate_r, own_i + mate_i),
        (own_r + turn_r, own_i + turn_i),
        (own_r - mate_r, own_i - mate_i),
        (own_r - turn_r, own_i - turn_i),
    ]


def chan_sign(chan_ref):
    return (1 - 2 * lax.rem(chan_ref[0], 2)).astype(f32)


def part_kernel(chan_ref, first_ref, twist_ref, last_ref, own_ref, mate_ref, *refs):
    outs, real_scratch, imag_scratch = refs[:2], refs[2], refs[3]
    group = real_scratch.shape[0]
    kept = last_ref.shape[0] // 4
    sign = chan_sign(chan_ref)

    def body(step, carry):
        for far in range(2):
            own = load_pair(own_ref.at[far], step * group, group)
            mate = load_pair(mate_ref.at[far], step * group, group)
            mixed = mix_two(own, mate, sign)
            results = transform(mixed, first_ref, twist_ref, last_ref, real_scratch, imag_scratch)
            for g, (real, imag) in enumerate(results):
                outs[far][step * group + g, :kept] = real.astype(bf16)
                outs[far][step * group + g, kept:] = imag.astype(bf16)
        return carry

    lax.fori_loop(0, own_ref.shape[1] // group, body, 0)


def final_kernel(scale, offset, chan_ref, join_ref, first_ref, twist_ref, last_ref, *refs):
    own_ref, mate_ref, near_ref, far_ref = refs[:4]
    out_ref, real_scratch, imag_scratch, staged, sem = refs[-5:]
    total = own_ref.shape[0]
    group = real_scratch.shape[0]
    kept = last_ref.shape[0] // 4
    sign = chan_sign(chan_ref)
    join_r, join_i = join_ref[chan_ref[0], 0], join_ref[chan_ref[0], 1]

    def body(step, carry):
        own = load_pair(own_ref, step * group, group)
        mate = load_pair(mate_ref, step * group, group)
        mixed = mix_two(own, mate, sign)
        results = transform(mixed, first_ref, twist_ref, last_ref, real_scratch, imag_scratch)
        for g, (real, imag) in enumerate(results):
            index = step * group + g
            other = near_ref[index].astype(f32) + far_ref[index].astype(f32)
            other_r, other_i = other[:kept], other[kept:]
            real = real + (other_r * join_r - other_i * join_i)
            imag = imag + (other_r * join_i + other_i * join_r)
            put_power(staged, index, real, imag, scale)
        return carry

    lax.fori_loop(0, total // group, body, 0)
    copy = pltpu.make_async_copy(staged, out_ref.at[pl.ds(offset, total)], sem)
    copy.start()
    copy.wait()


def delay_tables(channels, kept_rows, n_src):
    outer = channels // LANES
    local = outer // n_src
    firsts, twists = [], []
    for low_digit in range(n_src):
        d = n_src * np.arange(local) + low_digit
        cos1, sin1 = np_phase(d, np.arange(local), outer)
        high, low = np_split(np.block([[cos1, sin1], [-sin1, cos1]]))
        firsts.append(np.block([[high, high], [low, np.zeros_like(low)]]))
        twists.append(np.stack(np_phase(d, np.arange(LANES), channels)))
    first = np.stack(firsts)
    twist = np.stack(twists, axis=1).astype(np.float32)
    kept = np.arange(-(kept_rows // 2), kept_rows - kept_rows // 2)
    cos2, sin2 = np_phase(kept, np.arange(LANES), LANES)
    high, low = np_split(np.block([[cos2, sin2], [-sin2, cos2]]))
    last = np.concatenate([high, low], axis=0)
    return tuple(jnp.asarray(table) for table in (first, twist, last))


def join_table(outer):
    d = np.arange(outer)
    angle = np.stack([2 * d, -d, d, 2 * d])[:, None, None, :] * (math.pi / 2)
    return jnp.asarray(np.round(np.concatenate([np.cos(angle), np.sin(angle)], axis=1)).astype(np.float32))


def group_of(size):
    return max(g for g in range(1, GROUP_LIMIT + 1) if size % g == 0)


def transform_scratch(common, size):
    return [pltpu.VMEM((group_of(size), common["outer"], LANES), f32)] * 2


def powers(common, kernel, scalars, operands, previous, size):
    lane_rows = common["kept"] * common["outer"] // LANES
    arrays = list(common["tables"]) + list(operands)
    extra = [] if previous is None else [previous]
    return pl.pallas_call(
        kernel,
        in_specs=[smem()] * len(scalars)
        + [vmem()] * len(arrays)
        + [pl.BlockSpec(memory_space=pl.ANY)] * len(extra),
        out_specs=pl.BlockSpec(memory_space=pl.ANY),
        out_shape=jax.ShapeDtypeStruct((common["count"], lane_rows, LANES), f32),
        scratch_shapes=transform_scratch(common, size)
        + [pltpu.VMEM((size, lane_rows, LANES), f32), pltpu.SemaphoreType.DMA(())],
        input_output_aliases={len(scalars) + len(arrays): 0} if extra else {},
        cost_estimate=cost(5),
        compiler_params=kernel_params(),
    )(*scalars, *arrays, *extra)


def partials(common, own, mate):
    size = own.shape[1]
    shape = jax.ShapeDtypeStruct((size, 2 * common["kept"], common["outer"]), bf16)
    return pl.pallas_call(
        part_kernel,
        in_specs=[smem()] + [vmem()] * 5,
        out_specs=[vmem()] * 2,
        out_shape=[shape] * 2,
        scratch_shapes=transform_scratch(common, size),
        cost_estimate=cost(8),
        compiler_params=kernel_params(),
        name="partials",
    )(common["chan"], *common["tables"], own, mate)


def plan_for(count, n_chan):
    if n_chan == 4 and count == 60:
        return PLAN, ORDER
    chunks = 5 if count % 5 == 0 else 1
    order = [f"C{i}" for i in range(min(2, chunks))]
    for i in range(chunks):
        order.append(f"R{i}")
        if i + 2 < chunks:
            order.append(f"C{i + 2}")
    return [("A", count // chunks)] * chunks, order + [f"D{i}" for i in range(chunks)]


PLAN = [("A", 6), ("A", 8), ("H", 6), ("H", 8), ("A", 8), ("H", 8), ("H", 6), ("A", 10)]
ORDER = [
    "C0", "C2", "C1", "O0", "R0", "R2", "C3", "R1",
    "C4", "R3", "C5", "B2", "C6", "R4", "R5", "C7",
    "R6", "B3", "R7", "D4", "B5", "D0", "F3", "B6",
    "F2", "D7", "D1", "F5", "F6",
]


def shift_hops(n, shift):
    return [(j, (j + shift) % n) for j in range(n)]


def shards(samples, pcal_phase, tone_index, baseline_pairs):
    n_tm = lax.axis_size("tm")
    n_chan = lax.axis_size("chan")
    n_t, n_m = samples.shape[1:3]
    n_rates = n_t * n_tm
    assert n_rates == n_chan
    channels = samples.shape[5] * n_chan
    outer = channels // LANES
    kept_rows = N_DELAY // outer
    count = baseline_pairs.shape[0] // n_tm
    quant = 32767.0 / (18.0 * n_m * n_rates)
    scale = 1.0 / (100.0 * n_m * n_rates * channels) / (quant * quant)
    angles = two_pi * np.outer(np.arange(n_chan), np.arange(n_rates)) / n_rates
    turns = np.vectorize(clean)(np.stack([np.cos(angles), np.sin(angles)], axis=-1))
    levels, cal = prep(samples, tone_index, pcal_phase)
    common = {
        "n_tm": n_tm,
        "n_chan": n_chan,
        "count": count,
        "outer": outer,
        "kept": kept_rows,
        "quant": quant,
        "me": lax.axis_index("tm")[None],
        "chan": lax.axis_index("chan")[None],
        "pairs": baseline_pairs.T,
        "turns": jnp.asarray(turns.astype(np.float32).reshape(n_chan, 2 * n_rates)),
        "slots": jnp.asarray([0, 1, 1, 0], jnp.int32),
        "levels": levels,
        "cal": cal,
        "tables": delay_tables(channels, kept_rows, n_chan),
    }
    plan, order = plan_for(count, n_chan)
    offsets = [sum(size for _, size in plan[:i]) for i in range(len(plan))]
    received, own_vis, held, halves = {}, {}, {}, {}
    power = None
    for step in order:
        what, i = step[0], int(step[1:])
        (kind, size), offset = plan[i], offsets[i]
        if what == "C":
            shifts = list(range(1, n_tm)) + ([0] if f"O{i}" not in order else [])
            sent = correlate(common, offset, size, shifts)
            own_vis[i] = sent[n_tm - 1 :]
            received[i] = []
            for shift in range(1, n_tm):
                hops = shift_hops(n_tm, n_tm - shift)
                received[i].append(lax.ppermute(sent[shift - 1], "tm", hops))
        elif what == "O":
            own_vis[i] = correlate(common, offset, size, [0])
        elif what == "R":
            spectra = rates(common, list(own_vis[i]) + received[i], kind == "A")
            if kind == "A":
                held[i] = [spectra[0]]
                for shift in range(1, n_chan):
                    hops = shift_hops(n_chan, shift)
                    held[i].append(lax.ppermute(spectra[shift], "chan", hops))
            else:
                own, mate, two = spectra
                two_in = lax.ppermute(two, "chan", [(0, 1), (3, 2)])
                mate_in = lax.ppermute(mate, "chan", [(0, 1), (1, 0), (2, 3), (3, 2)])
                held[i] = [own, mate_in]
                halves[i] = [two, two_in]
        elif what == "B":
            near, far = partials(common, *halves[i])
            held[i].append(lax.ppermute(near, "chan", [(1, 2), (2, 1)]))
            held[i].append(lax.ppermute(far, "chan", [(1, 3), (2, 0)]))
        elif what == "D":
            kernel = functools.partial(delay_kernel, scale, offset, n_chan)
            power = powers(common, kernel, [], held[i], power, size)
        else:
            kernel = functools.partial(final_kernel_of, scale, offset)
            operands = held[i] + [join_table(outer)]
            power = powers(common, kernel, [common["chan"]], operands, power, size)
    return power.reshape(1, 1, count, N_DELAY)


def final_kernel_of(scale, offset, chan_ref, first_ref, twist_ref, last_ref, *refs):
    return final_kernel(
        scale, offset, chan_ref, refs[4], first_ref, twist_ref, last_ref, *refs[:4], *refs[5:]
    )


def solution(mesh):
    placed = (
        P("pol", ("scan", "tm"), None, None, None, "chan"),
        P("pol", None, None),
        P("chan"),
        P(),
    )
    return jax.shard_map(
        shards,
        mesh=mesh,
        in_specs=placed,
        out_specs=P("pol", ("scan", "chan"), "tm", None),
        check_vma=False,
    )
```

```python
import functools
import math

import jax
import jax.numpy as jnp
import numpy as np
from jax import lax
from jax.experimental import pallas as pl
from jax.experimental.pallas import tpu as pltpu
from jax.sharding import PartitionSpec as P


LANES = 128
NTONE = 128
N_DELAY = 8192
COST_SCALE = 2.0e6
VMEM_GRANT = 12 * 2**20
PREP_GRANT = 48 * 2**20
PREP_WIDTH = 2048
PAD = 1
GROUP_LIMIT = 14
two_pi = 2.0 * math.pi
bf16 = jnp.bfloat16
f32 = jnp.float32


def split_bf16(values):
    high = values.astype(bf16)
    return high, (values - high.astype(f32)).astype(bf16)


def np_split(values):
    values = np.asarray(values, np.float32)
    high = values.astype(bf16)
    return high, (values - high.astype(np.float32)).astype(bf16)


def np_phase(left, right, modulus):
    product = np.outer(left, right).astype(np.int64) % modulus
    angles = two_pi * product / modulus
    return np.cos(angles), np.sin(angles)


def prep_kernel(samples_ref, tone_ref, phase_ref, lev_ref, cal_ref, scratch):
    _, n_t, n_m, _, n_s, width = samples_ref.shape
    rows = width // LANES
    pitch = scratch.shape[0] // n_s

    def regroup(block):
        for row in range(rows):
            scratch[pl.ds(row, n_s, stride=pitch), :] = block[:, row * LANES : (row + 1) * LANES]
        return [scratch[s * pitch : s * pitch + rows, :] for s in range(n_s)]

    for t in range(n_t):
        for m in range(n_m):
            for p in range(2):
                level = (2 * samples_ref[0, t, m, p] - 3).astype(f32)
                for s, value in enumerate(regroup(level)):
                    lev_ref[t, m, p, s] = value.astype(bf16)
    slots = lax.broadcasted_iota(jnp.int32, (NTONE, width), 0)
    hot = jnp.where(slots == tone_ref[...], 1.0, 0.0).astype(bf16)
    for p, table in enumerate((jnp.cos(phase_ref[0]), jnp.sin(phase_ref[0]))):
        high, _ = split_bf16(table)
        middle, low = split_bf16(table - high.astype(f32))
        parts = jnp.concatenate([high, middle, low], axis=0)
        picked = jnp.dot(parts, hot, preferred_element_type=f32)
        total = (picked[:n_s] + picked[n_s : 2 * n_s]) + picked[2 * n_s :]
        for s, value in enumerate(regroup(total)):
            cal_ref[p, s] = value


def in_hbm(array):
    return pltpu.with_memory_space_constraint(array, pltpu.HBM)


def prep(samples, tone_index, pcal_phase):
    _, n_t, n_m, _, n_s, n_c = samples.shape
    width = min(n_c, PREP_WIDTH)
    rows = width // LANES
    return pl.pallas_call(
        prep_kernel,
        grid=(n_c // width,),
        in_specs=[
            pl.BlockSpec((1, n_t, n_m, 2, n_s, width), lambda i: (0, 0, 0, 0, 0, i)),
            pl.BlockSpec((1, width), lambda i: (0, i)),
            pl.BlockSpec((1, n_s, NTONE), lambda i: (0, 0, 0)),
        ],
        out_specs=[
            pl.BlockSpec((n_t, n_m, 2, n_s, rows, LANES), lambda i: (0, 0, 0, 0, i, 0)),
            pl.BlockSpec((2, n_s, rows, LANES), lambda i: (0, 0, i, 0)),
        ],
        out_shape=[
            jax.ShapeDtypeStruct((n_t, n_m, 2, n_s, n_c // LANES, LANES), bf16),
            jax.ShapeDtypeStruct((2, n_s, n_c // LANES, LANES), f32),
        ],
        scratch_shapes=[pltpu.VMEM((n_s * (rows + PAD), LANES), f32)],
        compiler_params=pltpu.CompilerParams(vmem_limit_bytes=PREP_GRANT),
        name="prep",
    )(samples, in_hbm(tone_index[None, :]), in_hbm(pcal_phase))


def visibility_rows(lev_ref, cal_ref, first, second, rows):
    n_t, n_m = lev_ref.shape[:2]
    cos_a, sin_a = cal_ref[0, first, rows], cal_ref[1, first, rows]
    cos_e, sin_e = cal_ref[0, second, rows], cal_ref[1, second, rows]
    cos_diff = cos_a * cos_e + sin_a * sin_e
    sin_diff = sin_a * cos_e - cos_a * sin_e
    result = []
    for t in range(n_t):
        real, imag = None, None
        for m in range(n_m):
            ar, ai = lev_ref[t, m, 0, first, rows], lev_ref[t, m, 1, first, rows]
            er, ei = lev_ref[t, m, 0, second, rows], lev_ref[t, m, 1, second, rows]
            re = ar * er + ai * ei
            im = ai * er - ar * ei
            real = re if real is None else real + re
            imag = im if imag is None else imag + im
        real, imag = real.astype(f32), imag.astype(f32)
        vis_real = real * cos_diff + imag * sin_diff
        vis_imag = imag * cos_diff - real * sin_diff
        result.append((vis_real.astype(bf16), vis_imag.astype(bf16)))
    return result


def vmem():
    return pl.BlockSpec(memory_space=pltpu.VMEM)


def smem():
    return pl.BlockSpec(memory_space=pltpu.SMEM)


def cost(micros):
    return pl.CostEstimate(flops=0, bytes_accessed=int(micros * COST_SCALE), transcendentals=0)


def corr_kernel(offset, count, shifts, n_tm, me_ref, pairs_ref, lev_ref, cal_ref, *outs):
    n_rows = lev_ref.shape[4]
    step = min(16, n_rows)
    starts = [lax.rem(me_ref[0] + (n_tm - s), n_tm) * count + offset for s in shifts]

    def body(index, carry):
        for start, out_ref in zip(starts, outs):
            first, second = pairs_ref[0, start + index], pairs_ref[1, start + index]
            for base in range(0, n_rows, step):
                rows = slice(base, base + step)
                for t, (real, imag) in enumerate(
                    visibility_rows(lev_ref, cal_ref, first, second, rows)
                ):
                    out_ref[index, t, 0, rows] = real
                    out_ref[index, t, 1, rows] = imag
        return carry

    lax.fori_loop(0, outs[0].shape[0], body, 0)


def kernel_params():
    return pltpu.CompilerParams(vmem_limit_bytes=VMEM_GRANT)


def correlate(common, offset, size, shifts):
    count, n_tm = common["count"], common["n_tm"]
    levels = common["levels"]
    shape = (size, levels.shape[0], 2) + levels.shape[4:]
    return pl.pallas_call(
        functools.partial(corr_kernel, offset, count, tuple(shifts), n_tm),
        in_specs=[smem(), smem(), vmem(), vmem()],
        out_specs=[vmem()] * len(shifts),
        out_shape=[jax.ShapeDtypeStruct(shape, bf16)] * len(shifts),
        cost_estimate=cost(3),
        compiler_params=kernel_params(),
        name="correlate",
    )(common["me"], common["pairs"], levels, common["cal"])


def weighted(terms):
    total = None
    for weight, value in terms:
        if weight == 0.0:
            continue
        value = value if abs(weight) == 1.0 else abs(weight) * value
        if total is None:
            total = value if weight > 0 else -value
        else:
            total = total + value if weight > 0 else total - value
    return total


def clean(value):
    rounded = round(value)
    return float(rounded) if abs(value - rounded) < 1e-12 else float(value)


def rate_kernel(quant, spread, chan_ref, turn_ref, slot_ref, *refs):
    n_rates = turn_ref.shape[1] // 2
    n_outs = n_rates if spread else 3
    blocks, outs = refs[:-n_outs], refs[-n_outs:]
    n_rows = blocks[0].shape[3]
    step = min(16, n_rows)
    chan = chan_ref[0]

    def body(index, carry):
        for base in range(0, n_rows, step):
            rows = slice(base, base + step)
            periods = []
            for ref in blocks:
                for t in range(ref.shape[1]):
                    periods.append((ref[index, t, 0, rows], ref[index, t, 1, rows]))
            turned = []
            for t, (real, imag) in enumerate(periods):
                real, imag = real.astype(f32), imag.astype(f32)
                if t == 0:
                    turned.append((real * quant, imag * quant))
                    continue
                cosine, sine = turn_ref[chan, 2 * t] * quant, turn_ref[chan, 2 * t + 1] * quant
                turned.append((real * cosine + imag * sine, imag * cosine - real * sine))
            spectrum = small_dft(turned)
            for p in range(2):
                values = [jnp.round(pair[p]).astype(jnp.int32) for pair in spectrum]
                if not spread:
                    even = lax.rem(chan, 2) == 0
                    values[1], values[3] = (
                        jnp.where(even, values[1], values[3]),
                        jnp.where(even, values[3], values[1]),
                    )
                values = [value.astype(jnp.int16) for value in values]
                if spread:
                    for value, out_ref in zip(values, outs):
                        out_ref[index, p, rows] = value
                    continue
                place = slot_ref[chan]
                outs[0][index, p, rows] = values[0]
                outs[1][index, p, rows] = values[1]
                outs[2][place, index, p, rows] = values[2]
                outs[2][1 - place, index, p, rows] = values[3]
        return carry

    lax.fori_loop(0, outs[0].shape[0], body, 0)


def small_dft(values):
    count = len(values)
    if count % 2 == 0:
        even, odd = small_dft(values[0::2]), small_dft(values[1::2])
        result = [None] * count
        for k in range(count // 2):
            angle = two_pi * k / count
            cosine, sine = clean(math.cos(angle)), clean(math.sin(angle))
            (er, ei), (odd_r, odd_i) = even[k], odd[k]
            tr = weighted([(cosine, odd_r), (sine, odd_i)])
            ti = weighted([(cosine, odd_i), (-sine, odd_r)])
            result[k] = (er + tr, ei + ti)
            result[k + count // 2] = (er - tr, ei - ti)
        return result
    result = []
    for k in range(count):
        real_terms, imag_terms = [], []
        for t, (real, imag) in enumerate(values):
            angle = two_pi * ((k * t) % count) / count
            cosine, sine = clean(math.cos(angle)), clean(math.sin(angle))
            real_terms += [(cosine, real), (sine, imag)]
            imag_terms += [(cosine, imag), (-sine, real)]
        result.append((weighted(real_terms), weighted(imag_terms)))
    return result


def rates(common, blocks, spread):
    size = blocks[0].shape[0]
    shape = (size, 2) + blocks[0].shape[3:]
    n_rates = common["n_chan"]
    shapes = [shape] * n_rates if spread else [shape, shape, (2,) + shape]
    return pl.pallas_call(
        functools.partial(rate_kernel, common["quant"], spread),
        in_specs=[smem()] * 3 + [vmem()] * len(blocks),
        out_specs=[vmem()] * len(shapes),
        out_shape=[jax.ShapeDtypeStruct(each, jnp.int16) for each in shapes],
        cost_estimate=cost(4),
        compiler_params=kernel_params(),
        name="rates",
    )(common["chan"], common["turns"], common["slots"], *blocks)


def load_pair(ref, index, group):
    return [
        jnp.concatenate(
            [ref[index + g, p].astype(jnp.int32).astype(f32) for g in range(group)], axis=1
        )
        for p in range(2)
    ]


def transform(mixed, first_ref, twist_ref, last_ref, real_scratch, imag_scratch):
    group = real_scratch.shape[0]
    n_src = len(mixed)
    rows = mixed[0][0].shape[0]
    for low_digit, (real, imag) in enumerate(mixed):
        real_parts, imag_parts = split_bf16(real), split_bf16(imag)
        stacked = jnp.concatenate(
            [real_parts[0], imag_parts[0], real_parts[1], imag_parts[1]], axis=0
        )
        both = jnp.dot(first_ref[low_digit], stacked, preferred_element_type=f32)
        section = both[: 2 * rows] + both[2 * rows :]
        twist_cos, twist_sin = twist_ref[0, low_digit], twist_ref[1, low_digit]
        for g in range(group):
            real = section[:rows, g * LANES : (g + 1) * LANES]
            imag = section[rows:, g * LANES : (g + 1) * LANES]
            place = pl.ds(low_digit, rows, stride=n_src)
            real_scratch[g, place, :] = real * twist_cos + imag * twist_sin
            imag_scratch[g, place, :] = imag * twist_cos - real * twist_sin
    kept = last_ref.shape[0] // 4
    results = []
    for g in range(group):
        operand = jnp.concatenate(
            [real_scratch[g].astype(bf16), imag_scratch[g].astype(bf16)], axis=1
        )
        both = lax.dot_general(
            last_ref[...], operand, (((1,), (1,)), ((), ())), preferred_element_type=f32
        )
        final = both[: 2 * kept] + both[2 * kept :]
        results.append((final[:kept], final[kept:]))
    return results


def put_power(staged, index, real, imag, scale):
    power = (real * real + imag * imag) * scale
    kept, outer = power.shape
    halves = outer // LANES
    for half in range(halves):
        place = pl.ds(half, kept, stride=halves)
        staged[index, place, :] = power[:, half * LANES : (half + 1) * LANES]


def delay_kernel(scale, offset, n_src, first_ref, twist_ref, last_ref, *refs):
    specs = refs[:n_src]
    out_ref, real_scratch, imag_scratch, staged, sem = refs[-5:]
    total = specs[0].shape[0]
    group = real_scratch.shape[0]

    def body(step, carry):
        sources = [tuple(load_pair(spec, step * group, group)) for spec in specs]
        mixed = small_dft([sources[0]] + sources[:0:-1])
        results = transform(mixed, first_ref, twist_ref, last_ref, real_scratch, imag_scratch)
        for g, (real, imag) in enumerate(results):
            put_power(staged, step * group + g, real, imag, scale)
        return carry

    lax.fori_loop(0, total // group, body, 0)
    copy = pltpu.make_async_copy(staged, out_ref.at[pl.ds(offset, total)], sem)
    copy.start()
    copy.wait()


def mix_two(own, mate, sign):
    (own_r, own_i), (mate_r, mate_i) = own, mate
    turn_r, turn_i = mate_i * sign, -(mate_r * sign)
    return [
        (own_r + mate_r, own_i + mate_i),
        (own_r + turn_r, own_i + turn_i),
        (own_r - mate_r, own_i - mate_i),
        (own_r - turn_r, own_i - turn_i),
    ]


def chan_sign(chan_ref):
    return (1 - 2 * lax.rem(chan_ref[0], 2)).astype(f32)


def part_kernel(chan_ref, first_ref, twist_ref, last_ref, own_ref, mate_ref, *refs):
    outs, real_scratch, imag_scratch = refs[:2], refs[2], refs[3]
    group = real_scratch.shape[0]
    kept = last_ref.shape[0] // 4
    sign = chan_sign(chan_ref)

    def body(step, carry):
        for far in range(2):
            own = load_pair(own_ref.at[far], step * group, group)
            mate = load_pair(mate_ref.at[far], step * group, group)
            mixed = mix_two(own, mate, sign)
            results = transform(mixed, first_ref, twist_ref, last_ref, real_scratch, imag_scratch)
            for g, (real, imag) in enumerate(results):
                outs[far][step * group + g, :kept] = real.astype(bf16)
                outs[far][step * group + g, kept:] = imag.astype(bf16)
        return carry

    lax.fori_loop(0, own_ref.shape[1] // group, body, 0)


def final_kernel(scale, offset, chan_ref, join_ref, first_ref, twist_ref, last_ref, *refs):
    own_ref, mate_ref, near_ref, far_ref = refs[:4]
    out_ref, real_scratch, imag_scratch, staged, sem = refs[-5:]
    total = own_ref.shape[0]
    group = real_scratch.shape[0]
    kept = last_ref.shape[0] // 4
    sign = chan_sign(chan_ref)
    join_r, join_i = join_ref[chan_ref[0], 0], join_ref[chan_ref[0], 1]

    def body(step, carry):
        own = load_pair(own_ref, step * group, group)
        mate = load_pair(mate_ref, step * group, group)
        mixed = mix_two(own, mate, sign)
        results = transform(mixed, first_ref, twist_ref, last_ref, real_scratch, imag_scratch)
        for g, (real, imag) in enumerate(results):
            index = step * group + g
            other = near_ref[index].astype(f32) + far_ref[index].astype(f32)
            other_r, other_i = other[:kept], other[kept:]
            real = real + (other_r * join_r - other_i * join_i)
            imag = imag + (other_r * join_i + other_i * join_r)
            put_power(staged, index, real, imag, scale)
        return carry

    lax.fori_loop(0, total // group, body, 0)
    copy = pltpu.make_async_copy(staged, out_ref.at[pl.ds(offset, total)], sem)
    copy.start()
    copy.wait()


def delay_tables(channels, kept_rows, n_src):
    outer = channels // LANES
    local = outer // n_src
    firsts, twists = [], []
    for low_digit in range(n_src):
        d = n_src * np.arange(local) + low_digit
        cos1, sin1 = np_phase(d, np.arange(local), outer)
        high, low = np_split(np.block([[cos1, sin1], [-sin1, cos1]]))
        firsts.append(np.block([[high, high], [low, np.zeros_like(low)]]))
        twists.append(np.stack(np_phase(d, np.arange(LANES), channels)))
    first = np.stack(firsts)
    twist = np.stack(twists, axis=1).astype(np.float32)
    kept = np.arange(-(kept_rows // 2), kept_rows - kept_rows // 2)
    cos2, sin2 = np_phase(kept, np.arange(LANES), LANES)
    high, low = np_split(np.block([[cos2, sin2], [-sin2, cos2]]))
    last = np.concatenate([high, low], axis=0)
    return tuple(jnp.asarray(table) for table in (first, twist, last))


def join_table(outer):
    d = np.arange(outer)
    angle = np.stack([2 * d, -d, d, 2 * d])[:, None, None, :] * (math.pi / 2)
    return jnp.asarray(np.round(np.concatenate([np.cos(angle), np.sin(angle)], axis=1)).astype(np.float32))


def group_of(size):
    return max(g for g in range(1, GROUP_LIMIT + 1) if size % g == 0)


def transform_scratch(common, size):
    return [pltpu.VMEM((group_of(size), common["outer"], LANES), f32)] * 2


def powers(common, kernel, scalars, operands, previous, size):
    lane_rows = common["kept"] * common["outer"] // LANES
    arrays = list(common["tables"]) + list(operands)
    extra = [] if previous is None else [previous]
    return pl.pallas_call(
        kernel,
        in_specs=[smem()] * len(scalars)
        + [vmem()] * len(arrays)
        + [pl.BlockSpec(memory_space=pl.ANY)] * len(extra),
        out_specs=pl.BlockSpec(memory_space=pl.ANY),
        out_shape=jax.ShapeDtypeStruct((common["count"], lane_rows, LANES), f32),
        scratch_shapes=transform_scratch(common, size)
        + [pltpu.VMEM((size, lane_rows, LANES), f32), pltpu.SemaphoreType.DMA(())],
        input_output_aliases={len(scalars) + len(arrays): 0} if extra else {},
        cost_estimate=cost(5),
        compiler_params=kernel_params(),
    )(*scalars, *arrays, *extra)


def partials(common, own, mate):
    size = own.shape[1]
    shape = jax.ShapeDtypeStruct((size, 2 * common["kept"], common["outer"]), bf16)
    return pl.pallas_call(
        part_kernel,
        in_specs=[smem()] + [vmem()] * 5,
        out_specs=[vmem()] * 2,
        out_shape=[shape] * 2,
        scratch_shapes=transform_scratch(common, size),
        cost_estimate=cost(8),
        compiler_params=kernel_params(),
        name="partials",
    )(common["chan"], *common["tables"], own, mate)


def plan_for(count, n_chan):
    if n_chan == 4 and count == 60:
        return PLAN, ORDER
    chunks = 5 if count % 5 == 0 else 1
    order = [f"C{i}" for i in range(min(2, chunks))]
    for i in range(chunks):
        order.append(f"R{i}")
        if i + 2 < chunks:
            order.append(f"C{i + 2}")
    return [("A", count // chunks)] * chunks, order + [f"D{i}" for i in range(chunks)]


PLAN = [("A", 6), ("A", 8), ("H", 6), ("H", 8), ("A", 10), ("H", 8), ("H", 6), ("A", 8)]
ORDER = [
    "C0", "C2", "C1", "O0", "R0", "R2", "C3", "R1",
    "C4", "R3", "C5", "B2", "C6", "R4", "R5", "C7",
    "R6", "B3", "R7", "D4", "D1", "B5", "D0", "F3",
    "B6", "F2", "D7", "F5", "F6",
]


def shift_hops(n, shift):
    return [(j, (j + shift) % n) for j in range(n)]


def shards(samples, pcal_phase, tone_index, baseline_pairs):
    n_tm = lax.axis_size("tm")
    n_chan = lax.axis_size("chan")
    n_t, n_m = samples.shape[1:3]
    n_rates = n_t * n_tm
    assert n_rates == n_chan
    channels = samples.shape[5] * n_chan
    outer = channels // LANES
    kept_rows = N_DELAY // outer
    count = baseline_pairs.shape[0] // n_tm
    quant = 32767.0 / (18.0 * n_m * n_rates)
    scale = 1.0 / (100.0 * n_m * n_rates * channels) / (quant * quant)
    angles = two_pi * np.outer(np.arange(n_chan), np.arange(n_rates)) / n_rates
    turns = np.vectorize(clean)(np.stack([np.cos(angles), np.sin(angles)], axis=-1))
    levels, cal = prep(samples, tone_index, pcal_phase)
    common = {
        "n_tm": n_tm,
        "n_chan": n_chan,
        "count": count,
        "outer": outer,
        "kept": kept_rows,
        "quant": quant,
        "me": lax.axis_index("tm")[None],
        "chan": lax.axis_index("chan")[None],
        "pairs": baseline_pairs.T,
        "turns": jnp.asarray(turns.astype(np.float32).reshape(n_chan, 2 * n_rates)),
        "slots": jnp.asarray([0, 1, 1, 0], jnp.int32),
        "levels": levels,
        "cal": cal,
        "tables": delay_tables(channels, kept_rows, n_chan),
    }
    plan, order = plan_for(count, n_chan)
    offsets = [sum(size for _, size in plan[:i]) for i in range(len(plan))]
    received, own_vis, held, halves = {}, {}, {}, {}
    power = None
    for step in order:
        what, i = step[0], int(step[1:])
        (kind, size), offset = plan[i], offsets[i]
        if what == "C":
            shifts = list(range(1, n_tm)) + ([0] if f"O{i}" not in order else [])
            sent = correlate(common, offset, size, shifts)
            own_vis[i] = sent[n_tm - 1 :]
            received[i] = []
            for shift in range(1, n_tm):
                hops = shift_hops(n_tm, n_tm - shift)
                received[i].append(lax.ppermute(sent[shift - 1], "tm", hops))
        elif what == "O":
            own_vis[i] = correlate(common, offset, size, [0])
        elif what == "R":
            spectra = rates(common, list(own_vis[i]) + received[i], kind == "A")
            if kind == "A":
                held[i] = [spectra[0]]
                for shift in range(1, n_chan):
                    hops = shift_hops(n_chan, shift)
                    held[i].append(lax.ppermute(spectra[shift], "chan", hops))
            else:
                own, mate, two = spectra
                two_in = lax.ppermute(two, "chan", [(0, 1), (3, 2)])
                mate_in = lax.ppermute(mate, "chan", [(0, 1), (1, 0), (2, 3), (3, 2)])
                held[i] = [own, mate_in]
                halves[i] = [two, two_in]
        elif what == "B":
            near, far = partials(common, *halves[i])
            held[i].append(lax.ppermute(near, "chan", [(1, 2), (2, 1)]))
            held[i].append(lax.ppermute(far, "chan", [(1, 3), (2, 0)]))
        elif what == "D":
            kernel = functools.partial(delay_kernel, scale, offset, n_chan)
            power = powers(common, kernel, [], held[i], power, size)
        else:
            kernel = functools.partial(final_kernel_of, scale, offset)
            operands = held[i] + [join_table(outer)]
            power = powers(common, kernel, [common["chan"]], operands, power, size)
    return power.reshape(1, 1, count, N_DELAY)


def final_kernel_of(scale, offset, chan_ref, first_ref, twist_ref, last_ref, *refs):
    return final_kernel(
        scale, offset, chan_ref, refs[4], first_ref, twist_ref, last_ref, *refs[:4], *refs[5:]
    )


def solution(mesh):
    placed = (
        P("pol", ("scan", "tm"), None, None, None, "chan"),
        P("pol", None, None),
        P("chan"),
        P(),
    )
    return jax.shard_map(
        shards,
        mesh=mesh,
        in_specs=placed,
        out_specs=P("pol", ("scan", "chan"), "tm", None),
        check_vma=False,
    )
```
